32 devices in a mesh: section: 4 (over x, core), row: 4 (over z), col: 2 (over y).
Axes of the slice: x: 2, y: 2, z: 4, core: 2. Of those that a mesh axis runs over, the one named last changes fastest.
Arguments:
- latents: bfloat16 [2, 1280, 4, 128], P(None, 'col', 'row'), may hold values from -6 to 6
- timesteps: int32 [2], replicated, may hold values from 0 to 999
- weights: bfloat16 [4, 1280, 1280], P('section', 'row', 'col'), may hold values from -0.15625 to 0.15625
- taps: float32 [4, 3, 1280], P('section'), may hold values from -3 to 3
- time_table: bfloat16 [4, 1000, 1280], P('section'), may hold values from -5 to 5
- dilations: int32 [4], P('section'), may hold values from 1 to 4
Outputs:
- acts: bfloat16 [4, 2, 1280, 4, 128], P('section', None, 'col', 'row')
The draws below stay inside these ranges and needn't reach their ends.
All inputs are finite; a program needn't handle non-finite values.
Results may differ from the reference program's by a relative error of at most 0.03.
Values may be sent and summed in bfloat16 or wider, within the bound.
A program may use at most 64 MiB of HBM per device.

```python
import jax
import jax.numpy as jnp
from jax import lax

CH = 1280
FRAMES = 128
MICRO = 2
NSTEPS = 1000
DMAX = 4
POSITIONS = 4
LEVELS = 4


def plant(values, stream_key, low, largest):
    longest = values.shape.index(max(values.shape))
    spots = []
    for shift in (0, 1):
        where = [jax.random.randint(jax.random.fold_in(stream_key, axis), (), 0, length) for axis, length in enumerate(values.shape)]
        where[longest] = (where[longest] + shift) % values.shape[longest]
        spots.append(tuple(where))
    return values.at[spots[0]].set(low).at[spots[1]].set(largest)


def block_scale(stream_key, extent, pieces, least, top_value):
    def one(dim, blocks):
        heights = jax.random.uniform(jax.random.fold_in(jax.random.fold_in(stream_key, 6), dim), (blocks,), jnp.float32, least / len(pieces), top_value / len(pieces))
        return jnp.repeat(jnp.exp(heights), extent[dim] // blocks).reshape((-1,) + (1,) * (len(extent) - dim - 1))

    level = one(*pieces[0])
    for cut in pieces[1:]:
        level = level * one(*cut)
    return level


def centred(own_key, dims, width, most, cuts=(), kind=jnp.bfloat16):
    entries = width * jax.random.normal(own_key, dims, jnp.float32)
    if cuts:
        entries = entries * block_scale(own_key, dims, cuts, -0.22, 0.18)
    return jnp.clip(entries, -most, most).astype(kind)


def setup_inputs(seed: int = 0) -> dict:
    key_list = jax.random.split(jax.random.key(seed), 7)
    return {
        "latents": centred(key_list[0], (MICRO, CH, POSITIONS, FRAMES), 1.0, 6.0, ((1, 2), (2, 4))),
        "timesteps": jax.random.randint(key_list[1], (MICRO,), 0, NSTEPS).astype(jnp.int32),
        "weights": centred(key_list[2], (LEVELS, CH, CH), CH ** -0.5, 0.15625, ((0, 4), (1, 4), (2, 2))),
        "taps": centred(key_list[3], (LEVELS, 3, CH), 0.6, 3.0, ((0, 4),), jnp.float32),
        "time_table": centred(key_list[4], (LEVELS, NSTEPS, CH), 1.0, 5.0, ((0, 4),)),
        "dilations": plant(jax.random.randint(key_list[5], (LEVELS,), 1, DMAX + 1), jax.random.fold_in(key_list[5], 1), 1, DMAX).astype(jnp.int32),
    }


def level_block(current, matrix, tap_rows, embedding, dilation, skip_term):
    widened = current.astype(jnp.float32)
    padded = jnp.pad(widened, ((0, 0), (0, 0), (DMAX, DMAX)))
    earlier = lax.dynamic_slice_in_dim(padded, (DMAX - dilation).astype(jnp.int32), FRAMES, 2)
    later_frames = lax.dynamic_slice_in_dim(padded, (DMAX + dilation).astype(jnp.int32), FRAMES, 2)
    summed = (tap_rows[0][:, None, None] * earlier + tap_rows[1][:, None, None] * widened
              + tap_rows[2][:, None, None] * later_frames + embedding[:, None, None])
    activated = jax.nn.silu(summed).astype(jnp.bfloat16)
    mixed = lax.dot_general(matrix, activated.reshape(CH, -1), (((0,), (0,)), ((), ())),
                            preferred_element_type=jnp.float32).reshape(widened.shape)
    return (widened + mixed + skip_term).astype(jnp.bfloat16)


def reference(latents, timesteps, weights, taps, time_table, dilations):
    results = [[None] * MICRO for level in range(LEVELS)]
    for micro_id in range(MICRO):
        current = latents[micro_id]
        for level in range(LEVELS):
            embedding = time_table[level, timesteps[micro_id]].astype(jnp.float32)
            if level >= LEVELS // 2:
                skip_term = results[LEVELS - 1 - level][micro_id].astype(jnp.float32)
            else:
                skip_term = jnp.float32(0.0)
            current = level_block(current, weights[level], taps[level], embedding,
                                  dilations[level], skip_term)
            results[level][micro_id] = current
    return jnp.stack([jnp.stack(row_list) for row_list in results])
```

```python
import functools

import jax
import jax.numpy as jnp
from jax import lax
from jax.experimental import pallas as pl
from jax.experimental.pallas import tpu as pltpu
from jax.sharding import PartitionSpec as P

MESH = pl.DeviceIdType.MESH
BLOCK = 640
CHUNK = 64
HOME = ((3, 3), (3, 3))


def kernel(
    counts,
    times_ref,
    dilation_ref,
    latent_hbm,
    weight_hbm,
    taps_hbm,
    table_hbm,
    out_ref,
    matrix,
    states,
    active,
    params,
    results,
    skips,
    table,
    latent_ref,
    taps_ref,
    local_sem,
    turn_sem,
    chunk_send,
    chunk_recv,
    lend_send,
    back_send,
    latent_send,
    state_send,
    state_recv,
    skip_send,
    skip_recv,
):
    sections, rows, cols = counts
    section = lax.axis_index("section")
    row = lax.axis_index("row")
    col = lax.axis_index("col")
    micro, width, frames = latent_ref.shape
    weight_ref = weight_hbm.at[0]
    depth = weight_ref.shape[0]
    steps = table.shape[0]
    middle = sections // 2
    mirror = sections - 1 - section
    blocks = [(low, min(low + BLOCK, width)) for low in range(0, width, BLOCK)]
    f32 = jnp.float32

    count = depth // CHUNK
    parity = lax.rem(section, 2)
    partner = jnp.where(section < middle, section + middle, section - middle)
    twin = jnp.where(parity == 0, section + 1, section - 1)
    at_end = jnp.logical_or(row == 0, row == rows - 1)

    def chunk(which, shard, q):
        return matrix.at[which, pl.ds(pl.multiple_of(shard * depth + q * CHUNK, 16), CHUNK)]

    own = pltpu.make_async_copy(weight_ref, matrix.at[0, pl.ds(pl.multiple_of(row * depth, 16), depth)], local_sem.at[0])
    own.start()
    fetch = pltpu.make_async_copy(table_hbm.at[0], table, local_sem.at[1])
    fetch.start()
    fetch_latents = pltpu.make_async_copy(latent_hbm, latent_ref, local_sem.at[2])
    fetch_latents.start()
    fetch_taps = pltpu.make_async_copy(taps_hbm, taps_ref, local_sem.at[3])
    fetch_taps.start()

    has_left, has_right = row > 0, row < rows - 1
    has_next, has_last = section < sections - 1, section > 0
    is_first = section == 0
    gives_skip, takes_skip = section < middle - 1, section > middle
    barrier = pltpu.get_barrier_semaphore()

    def greet(**where):
        pl.semaphore_signal(barrier, inc=1, device_id=where, device_id_type=MESH)

    @pl.when(has_left)
    def _():
        greet(row=row - 1)

    @pl.when(has_right)
    def _():
        greet(row=row + 1)

    @pl.when(has_next)
    def _():
        for other in range(cols):
            greet(section=section + 1, col=jnp.int32(other))

    @pl.when(has_last)
    def _():
        for other in range(cols):
            greet(section=section - 1, col=jnp.int32(other))

    @pl.when(is_first)
    def _():
        for hop in range(1, cols):
            greet(col=lax.rem(col + hop, cols))

    @pl.when(jnp.logical_or(gives_skip, takes_skip))
    def _():
        greet(section=mirror)

    greet(section=partner)

    def lends(step):
        there = row + step
        inside = jnp.logical_and(there >= 0, there < rows)
        edge = jnp.logical_or(at_end, jnp.logical_or(there == 0, there == rows - 1))
        return jnp.logical_and(inside, edge)

    for step in (-1, 1):

        @pl.when(lends(step))
        def _():
            greet(section=partner, row=row + step)

    def flag(condition):
        return condition.astype(jnp.int32)

    expected = (
        flag(has_left)
        + flag(has_right)
        + cols * (flag(has_next) + flag(has_last))
        + (cols - 1) * flag(is_first)
        + flag(jnp.logical_or(gives_skip, takes_skip))
        + 1
        + flag(lends(-1))
        + flag(lends(1))
    )
    pl.semaphore_wait(barrier, expected)

    def arrived(buffer, semaphore):
        pltpu.make_async_remote_copy(
            src_ref=buffer,
            dst_ref=buffer,
            send_sem=local_sem.at[0],
            recv_sem=semaphore,
            device_id={"row": row},
            device_id_type=MESH,
        ).wait_recv()

    def latent_copy(m, n, hop):
        low, high = blocks[n]
        block = states.at[m, col, :, pl.ds(low, high - low)]
        return pltpu.make_async_remote_copy(
            src_ref=block,
            dst_ref=block,
            send_sem=latent_send.at[m, n, hop],
            recv_sem=state_recv.at[m, n, col],
            device_id={"col": lax.rem(col + hop, cols)},
            device_id_type=MESH,
        )

    def state_copy(m, n, hop):
        low, high = blocks[n]
        return pltpu.make_async_remote_copy(
            src_ref=results.at[m, :, pl.ds(low, high - low)],
            dst_ref=states.at[m, col, :, pl.ds(low, high - low)],
            send_sem=state_send.at[m, n, hop],
            recv_sem=state_recv.at[m, n, col],
            device_id={"section": section + 1, "col": lax.rem(col + hop, cols)},
            device_id_type=MESH,
        )

    def skip_copy(m, n):
        low, high = blocks[n]
        return pltpu.make_async_remote_copy(
            src_ref=results.at[m, :, pl.ds(low, high - low)],
            dst_ref=skips.at[m, :, pl.ds(low, high - low)],
            send_sem=skip_send.at[m, n],
            recv_sem=skip_recv.at[m, n],
            device_id={"section": mirror},
            device_id_type=MESH,
        )

    fetch_latents.wait()

    @pl.when(is_first)
    def _():
        for m in range(micro):
            states[m, col] = latent_ref[m].astype(f32).T.astype(jnp.bfloat16)
            for hop in range(1, cols):
                for n in range(len(blocks)):
                    latent_copy(m, n, hop).start()

    @pl.when(section < middle)
    def _():
        skips[...] = jnp.zeros_like(skips)

    short = jnp.where(row < rows // 2, 1, -1)
    long = -short

    def move(helps, step, shard, q):
        there = row + step
        direct = jnp.logical_and(helps, jnp.logical_or(there == 0, there == rows - 1))
        which = helps.astype(jnp.int32)
        place = jnp.where(direct, 0, which)
        return pltpu.make_async_remote_copy(
            src_ref=chunk(which, shard, q),
            dst_ref=chunk(place, shard, q),
            send_sem=chunk_send.at[which, (step + 1) // 2, shard, q],
            recv_sem=chunk_recv.at[place, shard, q],
            device_id={"section": jnp.where(direct, partner, section), "row": there},
            device_id_type=MESH,
        )

    def lend(q):
        return pltpu.make_async_remote_copy(
            src_ref=chunk(0, row, q),
            dst_ref=chunk(1, row, q),
            send_sem=lend_send.at[q],
            recv_sem=chunk_recv.at[1, row, q],
            device_id={"section": partner},
            device_id_type=MESH,
        )

    def back(shard, q):
        return pltpu.make_async_remote_copy(
            src_ref=chunk(1, shard, q),
            dst_ref=chunk(0, shard, q),
            send_sem=back_send.at[shard, q],
            recv_sem=chunk_recv.at[0, shard, q],
            device_id={"section": partner},
            device_id_type=MESH,
        )

    def each(low, high, action):
        def one(q, carry):
            action(q)
            return carry

        lax.fori_loop(low, high, one, 0)

    def inside(index):
        return jnp.logical_and(index >= 0, index < rows)

    def got(which, shard, q):
        arrived(chunk(which, shard, q), chunk_recv.at[which, shard, q])

    def reach(step):
        return jnp.where(step > 0, row, rows - 1 - row)

    def share(turn):
        return jnp.where(parity == 0, HOME[turn][0], HOME[turn][1])

    def gather(turn, beside):
        helps = (section >= middle) if turn == 0 else (section < middle)
        which = helps.astype(jnp.int32)
        kept = share(turn)
        low, high = jnp.where(helps, kept, 0), jnp.where(helps, count, kept)

        @pl.when(jnp.logical_not(helps))
        def _():
            each(kept, count, lambda q: lend(q).start())

        for step in (short, long):

            @pl.when(jnp.logical_and(inside(row + step), jnp.logical_or(turn > 0, parity == 1)))
            def _():
                pl.semaphore_wait(turn_sem.at[(step + 1) // 2], 1)

        def first(q):
            @pl.when(helps)
            def _():
                got(1, row, q)

            for step in (short, long):

                @pl.when(inside(row + step))
                def _():
                    move(helps, step, row, q).start()

        each(low, high, first)

        for hop in range(rows):
            if hop > 0:
                for step in (long, short):
                    shard = row - step * hop

                    @pl.when(jnp.logical_and(inside(shard), jnp.logical_not(jnp.logical_and(helps, at_end))))
                    def _():
                        def onward(q):
                            got(which, shard, q)

                            @pl.when(inside(row + step))
                            def _():
                                move(helps, step, shard, q).start()

                            @pl.when(helps)
                            def _():
                                back(shard, q).start()

                        each(low, high, onward)

            for step in (short, long):

                @pl.when(jnp.logical_and(inside(row + step), reach(step) == hop))
                def _():
                    for past in range(hop + 1):
                        each(low, high, lambda q: move(helps, step, row - step * past, q).wait_send())
                    if turn == 0:
                        pl.semaphore_signal(
                            turn_sem.at[(step + 1) // 2], inc=1, device_id={"section": twin}, device_id_type=MESH
                        )
                    else:

                        @pl.when(parity == 0)
                        def _():
                            pl.semaphore_signal(
                                turn_sem.at[(step + 1) // 2], inc=1, device_id={"section": twin}, device_id_type=MESH
                            )

            beside(hop)

        @pl.when(jnp.logical_not(helps))
        def _():
            for hop in range(1, rows):
                shard = lax.rem(row + hop, rows)
                each(kept, count, lambda q: got(0, shard, q))

    def activate(m, is_latent):
        for n, (low, high) in enumerate(blocks):
            for hop in range(cols):
                other = lax.rem(col + hop, cols)
                if not (is_latent and hop == 0):
                    arrived(
                        states.at[m, other, :, pl.ds(low, high - low)],
                        state_recv.at[m, n, other],
                    )
                value = states[m, other, :, low:high]
                moved = jnp.dot(held[0], value, preferred_element_type=f32)
                half = (
                    params[other, 0:1, low:high] * moved[:frames]
                    + params[other, 1:2, low:high] * value.astype(f32)
                    + params[other, 2:3, low:high] * moved[frames:]
                    + params[other, 3 + m : 4 + m, low:high]
                )
                active[m, other, :, low:high] = (half + half * jnp.tanh(half)).astype(
                    jnp.bfloat16
                )

    own.wait()

    held = []

    def beside(hop):
        if hop == 0:
            dilation = dilation_ref[0]
            line = lax.broadcasted_iota(jnp.int32, (2 * frames, frames), 0)
            origin = lax.broadcasted_iota(jnp.int32, (2 * frames, frames), 1)
            wanted = jnp.where(line < frames, line - dilation, line - frames + dilation)
            shift = jnp.where(origin == wanted, 1.0, 0.0).astype(jnp.bfloat16)

            slot = lax.broadcasted_iota(jnp.int32, (16, steps), 0)
            number = lax.broadcasted_iota(jnp.int32, (16, steps), 1)
            chosen = jnp.zeros((16, steps), f32)
            for m in range(micro):
                hit = jnp.logical_and(slot == m, number == times_ref[m])
                chosen = jnp.where(hit, 1.0, chosen)
            fetch.wait()
            fetch_taps.wait()
            embedding = jnp.dot(chosen.astype(jnp.bfloat16), table[...], preferred_element_type=f32)
            for other in range(cols):
                span = slice(other * width, (other + 1) * width)
                for tap in range(3):
                    params[other, tap : tap + 1, :] = 0.5 * taps_ref[tap, :, span]
                params[other, 3 : 3 + micro, :] = 0.5 * embedding[0:micro, span]
            held.append(shift)
        if hop == 1:

            @pl.when(is_first)
            def _():
                for m in range(micro):
                    activate(m, True)

    def level():
        for m in range(micro):

            @pl.when(has_last)
            def _():
                activate(m, False)

            @pl.when(section == middle)
            def _():
                skips[m] = states[m, col]

            for n, (low, high) in enumerate(blocks):
                mixed = jnp.dot(
                    active[m, 0], matrix[0, 0:width, low:high], preferred_element_type=f32
                )
                for other in range(1, cols):
                    mixed += jnp.dot(
                        active[m, other],
                        matrix[0, other * width : (other + 1) * width, low:high],
                        preferred_element_type=f32,
                    )

                @pl.when(takes_skip)
                def _():
                    arrived(skips.at[m, :, pl.ds(low, high - low)], skip_recv.at[m, n])

                results[m, :, low:high] = (
                    states[m, col, :, low:high].astype(f32)
                    + mixed
                    + skips[m, :, low:high].astype(f32)
                ).astype(jnp.bfloat16)

                @pl.when(has_next)
                def _():
                    for hop in range(cols):
                        state_copy(m, n, hop).start()

                @pl.when(gives_skip)
                def _():
                    skip_copy(m, n).start()

    gather(0, beside)

    @pl.when(section < middle)
    def _():
        level()

    gather(1, lambda hop: None)

    @pl.when(section >= middle)
    def _():
        level()

    for m in range(micro):
        out_ref[m] = results[m].astype(f32).T.astype(jnp.bfloat16)

    @pl.when(is_first)
    def _():
        for m in range(micro):
            for hop in range(1, cols):
                for n in range(len(blocks)):
                    latent_copy(m, n, hop).wait_send()

    @pl.when(has_next)
    def _():
        for m in range(micro):
            for hop in range(cols):
                for n in range(len(blocks)):
                    state_copy(m, n, hop).wait_send()

    @pl.when(gives_skip)
    def _():
        for m in range(micro):
            for n in range(len(blocks)):
                skip_copy(m, n).wait_send()

    each(jnp.where(section < middle, share(0), share(1)), count, lambda q: lend(q).wait_send())

    @pl.when(jnp.logical_not(at_end))
    def _():
        for hop in range(1, rows):
            shard = lax.rem(row + hop, rows)
            each(jnp.where(section < middle, share(1), share(0)), count, lambda q: back(shard, q).wait_send())


def per_device(counts, latents, timesteps, weights, taps, time_table, dilations):
    sections, rows, cols = counts
    micro, width, _, frames = latents.shape
    depth = weights.shape[1]
    steps, channels = time_table.shape[1:]
    count = pl.cdiv(width, BLOCK)
    pieces = depth // CHUNK
    bf16 = jnp.bfloat16
    dma = pltpu.SemaphoreType.DMA
    vmem = pl.BlockSpec(memory_space=pltpu.VMEM)
    smem = pl.BlockSpec(memory_space=pltpu.SMEM)
    hbm = pl.BlockSpec(memory_space=pl.ANY)
    out = pl.pallas_call(
        functools.partial(kernel, counts),
        out_shape=jax.ShapeDtypeStruct((micro, width, frames), bf16),
        in_specs=[smem, smem, hbm, hbm, hbm, hbm],
        out_specs=vmem,
        scratch_shapes=[
            pltpu.VMEM((2, channels, width), bf16),
            pltpu.VMEM((micro, cols, frames, width), bf16),
            pltpu.VMEM((micro, cols, frames, width), bf16),
            pltpu.VMEM((cols, 8, width), jnp.float32),
            pltpu.VMEM((micro, frames, width), bf16),
            pltpu.VMEM((micro, frames, width), bf16),
            pltpu.VMEM((steps, channels), bf16),
            pltpu.VMEM((micro, width, frames), bf16),
            pltpu.VMEM((3, 1, channels), jnp.float32),
            dma((4,)),
            pltpu.SemaphoreType.REGULAR((2,)),
            dma((2, 2, rows, pieces)),
            dma((2, rows, pieces)),
            dma((pieces,)),
            dma((rows, pieces)),
            dma((micro, count, cols)),
            dma((micro, count, cols)),
            dma((micro, count, cols)),
            dma((micro, count)),
            dma((micro, count)),
        ],
        compiler_params=pltpu.CompilerParams(
            collective_id=0, has_side_effects=True, vmem_limit_bytes=60 * 2**20
        ),
    )(
        timesteps,
        dilations,
        latents.reshape(micro, width, frames),
        weights,
        taps.reshape(3, 1, channels),
        time_table,
    )
    return out.reshape(1, micro, width, 1, frames)


def solution(mesh):
    counts = tuple(mesh.shape[axis] for axis in ("section", "row", "col"))
    in_specs = (
        P(None, "col", "row", None),
        P(),
        P("section", "row", "col"),
        P("section", None, None),
        P("section", None, None),
        P("section"),
    )
    return jax.shard_map(
        functools.partial(per_device, counts),
        mesh=mesh,
        in_specs=in_specs,
        out_specs=P("section", None, "col", "row", None),
        check_vma=False,
    )
```

```python
import functools

import jax
import jax.numpy as jnp
from jax import lax
from jax.experimental import pallas as pl
from jax.experimental.pallas import tpu as pltpu
from jax.sharding import PartitionSpec as P

MESH = pl.DeviceIdType.MESH


def lanes_of(width):
    return 128 if width % 128 == 0 else width


def kept_of(blocks):
    return -(-3 * blocks // 5)


def kernel(
    counts,
    times_ref,
    dilation_ref,
    latent_hbm,
    weight_hbm,
    taps_hbm,
    table_hbm,
    out_ref,
    matrix,
    states,
    active,
    results,
    skips,
    params,
    shifts,
    table,
    latent_ref,
    taps_ref,
    local_sem,
    own_sem,
    turn_sem,
    chunk_send,
    chunk_recv,
    forward_send,
    lend_send,
    latent_send,
    state_send,
    state_recv,
    skip_send,
    skip_recv,
    out_send,
    out_recv,
    param_send,
    param_recv,
):
    sections, rows, cols = counts
    section = lax.axis_index("section")
    row = lax.axis_index("row")
    col = lax.axis_index("col")
    micro, width, frames = latent_ref.shape
    weight_ref = weight_hbm.at[0]
    depth = weight_ref.shape[0]
    steps = table.shape[0]
    middle = sections // 2
    lanes = lanes_of(width)
    blocks = width // lanes
    kept = kept_of(blocks)
    f32 = jnp.float32
    bf16 = jnp.bfloat16

    half = section // middle
    base = lax.rem(section, middle)
    partner = lax.rem(section + middle, sections)
    parity = lax.rem(base, 2)
    twin = jnp.where(parity == 0, section + 1, section - 1)
    mirror = middle - 1 - base + (1 - half) * middle
    next_base = lax.rem(base + 1, middle)
    last_base = lax.rem(base + middle - 1, middle)
    is_first = base == 0
    is_last = base == middle - 1

    def remote(source, target, send, recv, **where):
        return pltpu.make_async_remote_copy(
            src_ref=source, dst_ref=target, send_sem=send, recv_sem=recv, device_id=where, device_id_type=MESH
        )

    def arrived(buffer, semaphore):
        remote(buffer, buffer, local_sem.at[0], semaphore, row=row).wait_recv()

    def each(low, high, action):
        def one(q, carry):
            action(q)
            return carry

        lax.fori_loop(low, high, one, 0)

    def inside(index):
        return jnp.logical_and(index >= 0, index < rows)

    def chunk(turn, shard, q):
        return matrix.at[turn, q, pl.ds(pl.multiple_of(shard * depth, 16), depth)]

    def own(q):
        return pltpu.make_async_copy(weight_ref.at[:, pl.ds(q * lanes, lanes)], chunk(half, row, q), own_sem.at[q])

    for q in range(blocks):
        own(q).start()
    fetch_latents = pltpu.make_async_copy(latent_hbm, latent_ref, local_sem.at[2])
    fetch_latents.start()
    fetch_taps = pltpu.make_async_copy(taps_hbm, taps_ref, local_sem.at[3])
    fetch_taps.start()
    fetch = pltpu.make_async_copy(table_hbm.at[0], table, local_sem.at[1])
    fetch.start()

    barrier = pltpu.get_barrier_semaphore()

    def greet(**where):
        pl.semaphore_signal(barrier, inc=1, device_id=where, device_id_type=MESH)

    reach = [d for d in range(1, rows) if d < rows - 1 or rows == 2]
    strides = sorted((sign * d for d in reach for sign in (1, -1)), key=lambda d: (abs(d) != 2, abs(d)))
    at_end = jnp.logical_or(row == 0, row == rows - 1)
    passes = jnp.logical_and(rows > 2, jnp.logical_or(row == 1, row == rows - 2))
    far = jnp.where(row == 1, rows - 1, 0)
    onto = jnp.where(row == 1, 0, rows - 1)

    expected = jnp.int32(0)
    for d in strides:

        @pl.when(inside(row + d))
        def _():
            greet(row=row + d)

        expected += inside(row + d).astype(jnp.int32)

    greet(section=partner)
    expected += 1
    for other_base in (next_base,) if middle == 2 else (next_base, last_base):
        for other_half in range(2):
            for other in range(cols):
                greet(section=other_base + other_half * middle, col=jnp.int32(other))
                expected += 1
    if middle > 2:
        greet(section=mirror)
        expected += 1

    @pl.when(is_first)
    def _():
        for hop in range(1, cols):
            greet(col=lax.rem(col + hop, cols))

    expected += (cols - 1) * is_first.astype(jnp.int32)
    pl.semaphore_wait(barrier, expected)

    for q in range(blocks):
        own(q).wait()

    def lend(q):
        return remote(
            chunk(half, row, q), chunk(half, row, q), lend_send.at[q], chunk_recv.at[half, row, q], section=partner
        )

    def latent_copy(m, hop):
        block = states.at[0, m, pl.ds(col * blocks, blocks)]
        return remote(
            block, block, latent_send.at[m, hop], state_recv.at[0, m, col * 2], col=lax.rem(col + hop, cols)
        )

    groups = tuple(part for part in ((0, kept), (kept, blocks)) if part[0] < part[1])

    def group(turn, part):
        low, high = groups[part]
        return lambda m: results.at[turn, m, pl.ds(low, high - low)]

    def state_copy(turn, part, m, other_half, hop):
        low, high = groups[part]
        later = jnp.where(is_last, 1, 0) if turn == 0 else 1
        return remote(
            group(turn, part)(m),
            states.at[later, m, pl.ds(col * blocks + low, high - low)],
            state_send.at[turn, m, other_half, hop],
            state_recv.at[later, m, col * 2 + part],
            section=next_base + other_half * middle,
            col=lax.rem(col + hop, cols),
        )

    def skip_copy(part, m):
        low, high = groups[part]
        return remote(
            group(0, part)(m), skips.at[m, pl.ds(low, high - low)], skip_send.at[m], skip_recv.at[m], section=mirror
        )

    def out_copy(turn, m):
        block = group(turn, 1)(m)
        return remote(block, block, out_send.at[m], out_recv.at[m], section=partner)

    def param_copy():
        return remote(params.at[half], params.at[half], param_send.at[0], param_recv.at[0], section=partner)

    def move(turn, d, q):
        block = chunk(turn, row, q)
        there = row + d
        return remote(
            block, block, chunk_send.at[turn, there, q], chunk_recv.at[turn, row, q], row=there
        )

    def forward(turn, q):
        block = chunk(turn, far, q)
        return remote(block, block, forward_send.at[turn, q], chunk_recv.at[turn, far, q], row=onto)

    def got(turn, shard, q):
        arrived(chunk(turn, shard, q), chunk_recv.at[turn, shard, q])

    def prepare():
        slot = lax.broadcasted_iota(jnp.int32, (16, steps), 0)
        number = lax.broadcasted_iota(jnp.int32, (16, steps), 1)
        chosen = jnp.zeros((16, steps), f32)
        for m in range(micro):
            hit = jnp.logical_and(slot == m, number == times_ref[m])
            chosen = jnp.where(hit, 1.0, chosen)
        fetch.wait()
        fetch_taps.wait()
        embedding = jnp.dot(chosen.astype(bf16), table[...], preferred_element_type=f32)
        for tap in range(3):
            params[half, tap : tap + 1, :] = 0.5 * taps_ref[tap]
        params[half, 3 : 3 + micro, :] = 0.5 * embedding[0:micro]
        params[half, 7:8, :] = jnp.full((1, cols * width), dilation_ref[0].astype(f32), f32)
        param_copy().start()

    def shift_of(turn):
        line = lax.broadcasted_iota(jnp.int32, (2 * frames, frames), 0).astype(f32)
        origin = lax.broadcasted_iota(jnp.int32, (2 * frames, frames), 1).astype(f32)
        dilation = params[turn, 7:8, 0:frames]
        wanted = jnp.where(line < frames, line - dilation, line - frames + dilation)
        shifts[turn] = jnp.where(origin == wanted, 1.0, 0.0).astype(bf16)

    def bounds(turn):
        helps = half != turn
        return helps, jnp.where(helps, kept, 0), jnp.where(helps, blocks, kept)

    def to_each(d, soon):
        first = jnp.logical_or(at_end, abs(d) == 1)
        return jnp.logical_and(inside(row + d), first if soon else jnp.logical_not(first))

    def gather(turn):
        helps, low, high = bounds(turn)

        if turn == 0:

            @pl.when(parity == 1)
            def _():
                prepare()

                @pl.when(half == 0)
                def _():
                    each(kept, blocks, lambda q: lend(q).start())

        @pl.when(jnp.logical_or(turn > 0, parity == 1))
        def _():
            pl.semaphore_wait(turn_sem, 1)

        def first(q):
            @pl.when(helps)
            def _():
                got(turn, row, q)

            for d in strides:

                @pl.when(to_each(d, True))
                def _():
                    move(turn, d, q).start()

        each(low, high, first)

        if turn == 0:

            @pl.when(parity == 0)
            def _():
                prepare()

        def second(q):
            for d in strides:

                @pl.when(to_each(d, True))
                def _():
                    move(turn, d, q).wait_send()

            for d in strides:

                @pl.when(to_each(d, False))
                def _():
                    move(turn, d, q).start()

        each(low, high, second)

        @pl.when(jnp.logical_or(turn == 0, parity == 0))
        def _():
            pl.semaphore_signal(turn_sem, inc=1, device_id={"section": twin}, device_id_type=MESH)

        @pl.when(passes)
        def _():
            def onward(q):
                got(turn, far, q)
                forward(turn, q).start()

            each(low, high, onward)

        for hop in range(1, rows):
            shard = lax.rem(row + hop, rows)

            @pl.when(jnp.logical_not(jnp.logical_and(passes, shard == far)))
            def _():
                each(low, high, lambda q: got(turn, shard, q))

    def level(turn):
        helps, low, high = bounds(turn)

        @pl.when(helps)
        def _():
            arrived(params.at[turn], param_recv.at[0])

        shift_of(turn)

        def clip(m, carry):
            if turn == 0:

                @pl.when(is_first)
                def _():
                    for hop in range(1, cols):
                        other = lax.rem(col + hop, cols)
                        arrived(states.at[0, m, pl.ds(other * blocks, blocks)], state_recv.at[0, m, other * 2])

            for other in range(cols):
                for part, (low, high) in enumerate(groups):
                    span = states.at[turn, m, pl.ds(other * blocks + low, high - low)]
                    if turn == 0:

                        @pl.when(jnp.logical_not(is_first))
                        def _():
                            arrived(span, state_recv.at[0, m, other * 2 + part])

                    else:
                        arrived(span, state_recv.at[1, m, other * 2 + part])

            for g in range(cols * blocks):
                part = slice(g * lanes, (g + 1) * lanes)
                value = states[turn, m, g]
                moved = jnp.dot(shifts[turn], value, preferred_element_type=f32)
                pulse = params[turn, 3:4, part]
                for other in range(1, micro):
                    pulse = jnp.where(m == other, params[turn, 3 + other : 4 + other, part], pulse)
                vhalf = (
                    params[turn, 0:1, part] * moved[:frames]
                    + params[turn, 1:2, part] * value.astype(f32)
                    + params[turn, 2:3, part] * moved[frames:]
                    + pulse
                )
                active[:, part] = (vhalf + vhalf * jnp.tanh(vhalf)).astype(bf16)

            if turn == 1:

                @pl.when(is_first)
                def _():
                    for q in range(blocks):
                        skips[m, q] = states[1, m, col * blocks + q]

            def mix(part):
                low, high = groups[part]
                if turn == 1:

                    @pl.when(jnp.logical_not(is_first))
                    def _():
                        arrived(skips.at[m, pl.ds(low, high - low)], skip_recv.at[m])

                for q in range(low, high):
                    total = jnp.dot(active[...], matrix[turn, q], preferred_element_type=f32)
                    total = total + states[turn, m, col * blocks + q].astype(f32)
                    if turn == 1:
                        total = total + skips[m, q].astype(f32)
                    results[turn, m, q] = total.astype(bf16)

                @pl.when(jnp.logical_or(turn == 0, jnp.logical_not(is_last)))
                def _():
                    for other_half in range(2):
                        for hop in range(cols):
                            state_copy(turn, part, m, other_half, hop).start()

                if part == 1:
                    out_copy(turn, m).start()
                if turn == 0:

                    @pl.when(jnp.logical_not(is_last))
                    def _():
                        skip_copy(part, m).start()

            if len(groups) > 1:

                @pl.when(helps)
                def _():
                    mix(1)

            @pl.when(jnp.logical_not(helps))
            def _():
                mix(0)

            return carry

        lax.fori_loop(0, micro, clip, 0)

    @pl.when(jnp.logical_not(jnp.logical_and(parity == 1, half == 0)))
    def _():
        each(kept, blocks, lambda q: lend(q).start())

    fetch_latents.wait()

    @pl.when(is_first)
    def _():
        for m in range(micro):
            turned = latent_ref[m].astype(f32).T.astype(bf16)
            for q in range(blocks):
                states[0, m, col * blocks + q] = turned[:, q * lanes : (q + 1) * lanes]
            for hop in range(1, cols):
                latent_copy(m, hop).start()

    gather(0)
    level(0)
    gather(1)
    level(1)

    for m in range(micro):
        if len(groups) > 1:
            arrived(results.at[half, m, pl.ds(kept, blocks - kept)], out_recv.at[m])
        for q in range(blocks):
            out_ref[m, q * lanes : (q + 1) * lanes, :] = results[half, m, q].astype(f32).T.astype(bf16)

    each(kept, blocks, lambda q: lend(q).wait_send())
    param_copy().wait_send()

    @pl.when(is_first)
    def _():
        for m in range(micro):
            for hop in range(1, cols):
                latent_copy(m, hop).wait_send()

    for turn in range(2):
        helps, low, high = bounds(turn)

        def settle(q):
            for d in strides:

                @pl.when(to_each(d, False))
                def _():
                    move(turn, d, q).wait_send()

            @pl.when(passes)
            def _():
                forward(turn, q).wait_send()

        each(low, high, settle)

        def drain(part):
            for m in range(micro):

                @pl.when(jnp.logical_or(turn == 0, jnp.logical_not(is_last)))
                def _():
                    for other_half in range(2):
                        for hop in range(cols):
                            state_copy(turn, part, m, other_half, hop).wait_send()

                if part == 1:
                    out_copy(turn, m).wait_send()
                if turn == 0:

                    @pl.when(jnp.logical_not(is_last))
                    def _():
                        skip_copy(part, m).wait_send()

        if len(groups) > 1:

            @pl.when(helps)
            def _():
                drain(1)

        @pl.when(jnp.logical_not(helps))
        def _():
            drain(0)


def per_device(counts, latents, timesteps, weights, taps, time_table, dilations):
    sections, rows, cols = counts
    micro, width, _, frames = latents.shape
    depth = weights.shape[1]
    steps, channels = time_table.shape[1:]
    lanes = lanes_of(width)
    blocks = width // lanes
    bf16 = jnp.bfloat16
    dma = pltpu.SemaphoreType.DMA
    vmem = pl.BlockSpec(memory_space=pltpu.VMEM)
    smem = pl.BlockSpec(memory_space=pltpu.SMEM)
    hbm = pl.BlockSpec(memory_space=pl.ANY)
    out = pl.pallas_call(
        functools.partial(kernel, counts),
        out_shape=jax.ShapeDtypeStruct((micro, width, frames), bf16),
        in_specs=[smem, smem, hbm, hbm, hbm, hbm],
        out_specs=vmem,
        scratch_shapes=[
            pltpu.VMEM((2, blocks, channels, lanes), bf16),
            pltpu.VMEM((2, micro, cols * blocks, frames, lanes), bf16),
            pltpu.VMEM((frames, channels), bf16),
            pltpu.VMEM((2, micro, blocks, frames, lanes), bf16),
            pltpu.VMEM((micro, blocks, frames, lanes), bf16),
            pltpu.VMEM((2, 8, channels), jnp.float32),
            pltpu.VMEM((2, 2 * frames, frames), bf16),
            pltpu.VMEM((steps, channels), bf16),
            pltpu.VMEM((micro, width, frames), bf16),
            pltpu.VMEM((3, 1, channels), jnp.float32),
            dma((4,)),
            dma((blocks,)),
            pltpu.SemaphoreType.REGULAR,
            dma((2, rows, blocks)),
            dma((2, rows, blocks)),
            dma((2, blocks)),
            dma((blocks,)),
            dma((micro, cols)),
            dma((2, micro, 2, cols)),
            dma((2, micro, cols * 2)),
            dma((micro,)),
            dma((micro,)),
            dma((micro,)),
            dma((micro,)),
            dma((1,)),
            dma((1,)),
        ],
        compiler_params=pltpu.CompilerParams(
            collective_id=0, has_side_effects=True, vmem_limit_bytes=60 * 2**20
        ),
    )(
        timesteps,
        dilations,
        latents.reshape(micro, width, frames),
        weights,
        taps.reshape(3, 1, channels),
        time_table,
    )
    return out.reshape(1, micro, width, 1, frames)


def solution(mesh):
    counts = tuple(mesh.shape[axis] for axis in ("section", "row", "col"))
    in_specs = (
        P(None, "col", "row", None),
        P(),
        P("section", "row", "col"),
        P("section", None, None),
        P("section", None, None),
        P("section"),
    )
    return jax.shard_map(
        functools.partial(per_device, counts),
        mesh=mesh,
        in_specs=in_specs,
        out_specs=P("section", None, "col", "row", None),
        check_vma=False,
    )
```

```python
import functools

import jax
import jax.numpy as jnp
from jax import lax
from jax.experimental import pallas as pl
from jax.experimental.pallas import tpu as pltpu
from jax.sharding import PartitionSpec as P

MESH = pl.DeviceIdType.MESH


def lanes_of(width):
    return 128 if width % 128 == 0 else width


def kept_of(blocks):
    return -(-3 * blocks // 5)


def kernel(
    counts,
    times_ref,
    dilation_ref,
    latent_hbm,
    weight_hbm,
    taps_hbm,
    table_hbm,
    out_ref,
    matrix,
    states,
    active,
    results,
    skips,
    params,
    shifts,
    table,
    latent_ref,
    taps_ref,
    local_sem,
    own_sem,
    turn_sem,
    chunk_send,
    chunk_recv,
    forward_send,
    lend_send,
    latent_send,
    state_send,
    state_recv,
    skip_send,
    skip_recv,
    out_send,
    out_recv,
    param_send,
    param_recv,
):
    sections, rows, cols = counts
    section = lax.axis_index("section")
    row = lax.axis_index("row")
    col = lax.axis_index("col")
    micro, width, frames = latent_ref.shape
    weight_ref = weight_hbm.at[0]
    depth = weight_ref.shape[0]
    steps = table.shape[0]
    middle = sections // 2
    lanes = lanes_of(width)
    blocks = width // lanes
    kept = kept_of(blocks)
    f32 = jnp.float32
    bf16 = jnp.bfloat16

    half = section // middle
    base = lax.rem(section, middle)
    partner = lax.rem(section + middle, sections)
    parity = lax.rem(base, 2)
    twin = jnp.where(parity == 0, section + 1, section - 1)
    mirror = middle - 1 - base + (1 - half) * middle
    next_base = lax.rem(base + 1, middle)
    last_base = lax.rem(base + middle - 1, middle)
    is_first = base == 0
    is_last = base == middle - 1

    def remote(source, target, send, recv, **where):
        return pltpu.make_async_remote_copy(
            src_ref=source, dst_ref=target, send_sem=send, recv_sem=recv, device_id=where, device_id_type=MESH
        )

    def arrived(buffer, semaphore):
        remote(buffer, buffer, local_sem.at[0], semaphore, row=row).wait_recv()

    def each(low, high, action):
        def one(q, carry):
            action(q)
            return carry

        lax.fori_loop(low, high, one, 0)

    def inside(index):
        return jnp.logical_and(index >= 0, index < rows)

    def chunk(turn, shard, q):
        return matrix.at[turn, q, pl.ds(pl.multiple_of(shard * depth, 16), depth)]

    def own(q):
        return pltpu.make_async_copy(weight_ref.at[:, pl.ds(q * lanes, lanes)], chunk(half, row, q), own_sem.at[q])

    for q in range(blocks):
        own(q).start()
    fetch_latents = pltpu.make_async_copy(latent_hbm, latent_ref, local_sem.at[2])
    fetch_latents.start()
    fetch_taps = pltpu.make_async_copy(taps_hbm, taps_ref, local_sem.at[3])
    fetch_taps.start()
    fetch = pltpu.make_async_copy(table_hbm.at[0], table, local_sem.at[1])
    fetch.start()

    barrier = pltpu.get_barrier_semaphore()

    def greet(**where):
        pl.semaphore_signal(barrier, inc=1, device_id=where, device_id_type=MESH)

    reach = [d for d in range(1, rows) if d < rows - 1 or rows == 2]
    strides = sorted((sign * d for d in reach for sign in (1, -1)), key=lambda d: (abs(d) != 2, abs(d)))
    at_end = jnp.logical_or(row == 0, row == rows - 1)
    passes = jnp.logical_and(rows > 2, jnp.logical_or(row == 1, row == rows - 2))
    far = jnp.where(row == 1, rows - 1, 0)
    onto = jnp.where(row == 1, 0, rows - 1)

    expected = jnp.int32(0)
    for d in strides:

        @pl.when(inside(row + d))
        def _():
            greet(row=row + d)

        expected += inside(row + d).astype(jnp.int32)

    greet(section=partner)
    expected += 1
    for other_base in (next_base,) if middle == 2 else (next_base, last_base):
        for other_half in range(2):
            for other in range(cols):
                greet(section=other_base + other_half * middle, col=jnp.int32(other))
                expected += 1
    if middle > 2:
        greet(section=mirror)
        expected += 1

    @pl.when(is_first)
    def _():
        for hop in range(1, cols):
            greet(col=lax.rem(col + hop, cols))

    expected += (cols - 1) * is_first.astype(jnp.int32)
    pl.semaphore_wait(barrier, expected)

    for q in range(blocks):
        own(q).wait()

    def lend(q):
        return remote(
            chunk(half, row, q), chunk(half, row, q), lend_send.at[q], chunk_recv.at[half, row, q], section=partner
        )

    def latent_copy(m, hop):
        block = states.at[0, m, pl.ds(col * blocks, blocks)]
        return remote(
            block, block, latent_send.at[m, hop], state_recv.at[0, m, col * 2], col=lax.rem(col + hop, cols)
        )

    groups = tuple(part for part in ((0, kept), (kept, blocks)) if part[0] < part[1])

    def group(turn, part):
        low, high = groups[part]
        return lambda m: results.at[turn, m, pl.ds(low, high - low)]

    def state_copy(turn, part, m, other_half, hop):
        low, high = groups[part]
        later = jnp.where(is_last, 1, 0) if turn == 0 else 1
        return remote(
            group(turn, part)(m),
            states.at[later, m, pl.ds(col * blocks + low, high - low)],
            state_send.at[turn, m, other_half, hop],
            state_recv.at[later, m, col * 2 + part],
            section=next_base + other_half * middle,
            col=lax.rem(col + hop, cols),
        )

    def skip_copy(part, m):
        low, high = groups[part]
        return remote(
            group(0, part)(m), skips.at[m, pl.ds(low, high - low)], skip_send.at[m], skip_recv.at[m], section=mirror
        )

    def out_copy(turn, m):
        block = group(turn, 1)(m)
        return remote(block, block, out_send.at[m], out_recv.at[m], section=partner)

    def param_copy():
        return remote(params.at[half], params.at[half], param_send.at[0], param_recv.at[0], section=partner)

    def move(turn, d, q):
        block = chunk(turn, row, q)
        there = row + d
        return remote(
            block, block, chunk_send.at[turn, there, q], chunk_recv.at[turn, row, q], row=there
        )

    def forward(turn, q):
        block = chunk(turn, far, q)
        return remote(block, block, forward_send.at[turn, q], chunk_recv.at[turn, far, q], row=onto)

    def got(turn, shard, q):
        arrived(chunk(turn, shard, q), chunk_recv.at[turn, shard, q])

    def prepare():
        slot = lax.broadcasted_iota(jnp.int32, (16, steps), 0)
        number = lax.broadcasted_iota(jnp.int32, (16, steps), 1)
        chosen = jnp.zeros((16, steps), f32)
        for m in range(micro):
            hit = jnp.logical_and(slot == m, number == times_ref[m])
            chosen = jnp.where(hit, 1.0, chosen)
        fetch.wait()
        fetch_taps.wait()
        embedding = jnp.dot(chosen.astype(bf16), table[...], preferred_element_type=f32)
        for tap in range(3):
            params[half, tap : tap + 1, :] = 0.5 * taps_ref[tap]
        params[half, 3 : 3 + micro, :] = 0.5 * embedding[0:micro]
        params[half, 7:8, :] = jnp.full((1, cols * width), dilation_ref[0].astype(f32), f32)
        param_copy().start()

    def shift_of(turn):
        line = lax.broadcasted_iota(jnp.int32, (2 * frames, frames), 0).astype(f32)
        origin = lax.broadcasted_iota(jnp.int32, (2 * frames, frames), 1).astype(f32)
        dilation = params[turn, 7:8, 0:frames]
        wanted = jnp.where(line < frames, line - dilation, line - frames + dilation)
        shifts[turn] = jnp.where(origin == wanted, 1.0, 0.0).astype(bf16)

    def bounds(turn):
        helps = half != turn
        return helps, jnp.where(helps, kept, 0), jnp.where(helps, blocks, kept)

    def to_each(d, soon):
        to_end = jnp.logical_or(row + d == 0, row + d == rows - 1)
        first = jnp.where(at_end, abs(d) != 1, to_end)
        return jnp.logical_and(inside(row + d), first if soon else jnp.logical_not(first))

    def gather(turn):
        helps, low, high = bounds(turn)

        if turn == 0:

            @pl.when(parity == 1)
            def _():
                prepare()

                @pl.when(half == 0)
                def _():
                    each(kept, blocks, lambda q: lend(q).start())

        @pl.when(jnp.logical_or(turn > 0, parity == 1))
        def _():
            pl.semaphore_wait(turn_sem, 1)

        def first(q):
            @pl.when(helps)
            def _():
                got(turn, row, q)

            for d in strides:

                @pl.when(to_each(d, True))
                def _():
                    move(turn, d, q).start()

        each(low, high, first)

        if turn == 0:

            @pl.when(parity == 0)
            def _():
                prepare()

        def second(q):
            for d in strides:

                @pl.when(to_each(d, True))
                def _():
                    move(turn, d, q).wait_send()

            for d in strides:

                @pl.when(to_each(d, False))
                def _():
                    move(turn, d, q).start()

        each(low, high, second)

        @pl.when(jnp.logical_or(turn == 0, parity == 0))
        def _():
            pl.semaphore_signal(turn_sem, inc=1, device_id={"section": twin}, device_id_type=MESH)

        @pl.when(passes)
        def _():
            def onward(q):
                got(turn, far, q)
                forward(turn, q).start()

            each(low, high, onward)

        for hop in range(1, rows):
            shard = lax.rem(row + hop, rows)

            @pl.when(jnp.logical_not(jnp.logical_and(passes, shard == far)))
            def _():
                each(low, high, lambda q: got(turn, shard, q))

    def level(turn):
        helps, low, high = bounds(turn)

        @pl.when(helps)
        def _():
            arrived(params.at[turn], param_recv.at[0])

        shift_of(turn)

        def clip(m, carry):
            if turn == 0:

                @pl.when(is_first)
                def _():
                    for hop in range(1, cols):
                        other = lax.rem(col + hop, cols)
                        arrived(states.at[0, m, pl.ds(other * blocks, blocks)], state_recv.at[0, m, other * 2])

            for other in range(cols):
                for part, (low, high) in enumerate(groups):
                    span = states.at[turn, m, pl.ds(other * blocks + low, high - low)]
                    if turn == 0:

                        @pl.when(jnp.logical_not(is_first))
                        def _():
                            arrived(span, state_recv.at[0, m, other * 2 + part])

                    else:
                        arrived(span, state_recv.at[1, m, other * 2 + part])

            for g in range(cols * blocks):
                part = slice(g * lanes, (g + 1) * lanes)
                value = states[turn, m, g]
                moved = jnp.dot(shifts[turn], value, preferred_element_type=f32)
                pulse = params[turn, 3:4, part]
                for other in range(1, micro):
                    pulse = jnp.where(m == other, params[turn, 3 + other : 4 + other, part], pulse)
                vhalf = (
                    params[turn, 0:1, part] * moved[:frames]
                    + params[turn, 1:2, part] * value.astype(f32)
                    + params[turn, 2:3, part] * moved[frames:]
                    + pulse
                )
                active[:, part] = (vhalf + vhalf * jnp.tanh(vhalf)).astype(bf16)

            if turn == 1:

                @pl.when(is_first)
                def _():
                    for q in range(blocks):
                        skips[m, q] = states[1, m, col * blocks + q]

            def mix(part):
                low, high = groups[part]
                if turn == 1:

                    @pl.when(jnp.logical_not(is_first))
                    def _():
                        arrived(skips.at[m, pl.ds(low, high - low)], skip_recv.at[m])

                for q in range(low, high):
                    total = jnp.dot(active[...], matrix[turn, q], preferred_element_type=f32)
                    total = total + states[turn, m, col * blocks + q].astype(f32)
                    if turn == 1:
                        total = total + skips[m, q].astype(f32)
                    results[turn, m, q] = total.astype(bf16)

                @pl.when(jnp.logical_or(turn == 0, jnp.logical_not(is_last)))
                def _():
                    for other_half in range(2):
                        for hop in range(cols):
                            state_copy(turn, part, m, other_half, hop).start()

                if part == 1:
                    out_copy(turn, m).start()
                if turn == 0:

                    @pl.when(jnp.logical_not(is_last))
                    def _():
                        skip_copy(part, m).start()

            if len(groups) > 1:

                @pl.when(helps)
                def _():
                    mix(1)

            @pl.when(jnp.logical_not(helps))
            def _():
                mix(0)

            return carry

        lax.fori_loop(0, micro, clip, 0)

    @pl.when(jnp.logical_not(jnp.logical_and(parity == 1, half == 0)))
    def _():
        each(kept, blocks, lambda q: lend(q).start())

    fetch_latents.wait()

    @pl.when(is_first)
    def _():
        for m in range(micro):
            turned = latent_ref[m].astype(f32).T.astype(bf16)
            for q in range(blocks):
                states[0, m, col * blocks + q] = turned[:, q * lanes : (q + 1) * lanes]
            for hop in range(1, cols):
                latent_copy(m, hop).start()

    gather(0)
    level(0)
    gather(1)
    level(1)

    for m in range(micro):
        if len(groups) > 1:
            arrived(results.at[half, m, pl.ds(kept, blocks - kept)], out_recv.at[m])
        for q in range(blocks):
            out_ref[m, q * lanes : (q + 1) * lanes, :] = results[half, m, q].astype(f32).T.astype(bf16)

    each(kept, blocks, lambda q: lend(q).wait_send())
    param_copy().wait_send()

    @pl.when(is_first)
    def _():
        for m in range(micro):
            for hop in range(1, cols):
                latent_copy(m, hop).wait_send()

    for turn in range(2):
        helps, low, high = bounds(turn)

        def settle(q):
            for d in strides:

                @pl.when(to_each(d, False))
                def _():
                    move(turn, d, q).wait_send()

            @pl.when(passes)
            def _():
                forward(turn, q).wait_send()

        each(low, high, settle)

        def drain(part):
            for m in range(micro):

                @pl.when(jnp.logical_or(turn == 0, jnp.logical_not(is_last)))
                def _():
                    for other_half in range(2):
                        for hop in range(cols):
                            state_copy(turn, part, m, other_half, hop).wait_send()

                if part == 1:
                    out_copy(turn, m).wait_send()
                if turn == 0:

                    @pl.when(jnp.logical_not(is_last))
                    def _():
                        skip_copy(part, m).wait_send()

        if len(groups) > 1:

            @pl.when(helps)
            def _():
                drain(1)

        @pl.when(jnp.logical_not(helps))
        def _():
            drain(0)


def per_device(counts, latents, timesteps, weights, taps, time_table, dilations):
    sections, rows, cols = counts
    micro, width, _, frames = latents.shape
    depth = weights.shape[1]
    steps, channels = time_table.shape[1:]
    lanes = lanes_of(width)
    blocks = width // lanes
    bf16 = jnp.bfloat16
    dma = pltpu.SemaphoreType.DMA
    vmem = pl.BlockSpec(memory_space=pltpu.VMEM)
    smem = pl.BlockSpec(memory_space=pltpu.SMEM)
    hbm = pl.BlockSpec(memory_space=pl.ANY)
    out = pl.pallas_call(
        functools.partial(kernel, counts),
        out_shape=jax.ShapeDtypeStruct((micro, width, frames), bf16),
        in_specs=[smem, smem, hbm, hbm, hbm, hbm],
        out_specs=vmem,
        scratch_shapes=[
            pltpu.VMEM((2, blocks, channels, lanes), bf16),
            pltpu.VMEM((2, micro, cols * blocks, frames, lanes), bf16),
            pltpu.VMEM((frames, channels), bf16),
            pltpu.VMEM((2, micro, blocks, frames, lanes), bf16),
            pltpu.VMEM((micro, blocks, frames, lanes), bf16),
            pltpu.VMEM((2, 8, channels), jnp.float32),
            pltpu.VMEM((2, 2 * frames, frames), bf16),
            pltpu.VMEM((steps, channels), bf16),
            pltpu.VMEM((micro, width, frames), bf16),
            pltpu.VMEM((3, 1, channels), jnp.float32),
            dma((4,)),
            dma((blocks,)),
            pltpu.SemaphoreType.REGULAR,
            dma((2, rows, blocks)),
            dma((2, rows, blocks)),
            dma((2, blocks)),
            dma((blocks,)),
            dma((micro, cols)),
            dma((2, micro, 2, cols)),
            dma((2, micro, cols * 2)),
            dma((micro,)),
            dma((micro,)),
            dma((micro,)),
            dma((micro,)),
            dma((1,)),
            dma((1,)),
        ],
        compiler_params=pltpu.CompilerParams(
            collective_id=0, has_side_effects=True, vmem_limit_bytes=60 * 2**20
        ),
    )(
        timesteps,
        dilations,
        latents.reshape(micro, width, frames),
        weights,
        taps.reshape(3, 1, channels),
        time_table,
    )
    return out.reshape(1, micro, width, 1, frames)


def solution(mesh):
    counts = tuple(mesh.shape[axis] for axis in ("section", "row", "col"))
    in_specs = (
        P(None, "col", "row", None),
        P(),
        P("section", "row", "col"),
        P("section", None, None),
        P("section", None, None),
        P("section"),
    )
    return jax.shard_map(
        functools.partial(per_device, counts),
        mesh=mesh,
        in_specs=in_specs,
        out_specs=P("section", None, "col", "row", None),
        check_vma=False,
    )
```

```python
import functools

import jax
import jax.numpy as jnp
from jax import lax
from jax.experimental import pallas as pl
from jax.experimental.pallas import tpu as pltpu
from jax.sharding import PartitionSpec as P

MESH = pl.DeviceIdType.MESH


def lanes_of(width):
    return 128 if width % 128 == 0 else width


def kept_of(blocks):
    return -(-3 * blocks // 5)


def kernel(
    counts,
    times_ref,
    dilation_ref,
    latent_hbm,
    weight_hbm,
    taps_hbm,
    table_hbm,
    out_ref,
    matrix,
    states,
    active,
    results,
    skips,
    params,
    shifts,
    table,
    latent_ref,
    taps_ref,
    local_sem,
    own_sem,
    turn_sem,
    chunk_send,
    chunk_recv,
    forward_send,
    lend_send,
    latent_send,
    state_send,
    state_recv,
    skip_send,
    skip_recv,
    out_send,
    out_recv,
    param_send,
    param_recv,
):
    sections, rows, cols = counts
    section = lax.axis_index("section")
    row = lax.axis_index("row")
    col = lax.axis_index("col")
    micro, width, frames = latent_ref.shape
    weight_ref = weight_hbm.at[0]
    depth = weight_ref.shape[0]
    steps = table.shape[0]
    middle = sections // 2
    lanes = lanes_of(width)
    blocks = width // lanes
    kept = kept_of(blocks)
    f32 = jnp.float32
    bf16 = jnp.bfloat16

    half = section // middle
    base = lax.rem(section, middle)
    partner = lax.rem(section + middle, sections)
    parity = lax.rem(base, 2)
    twin = jnp.where(parity == 0, section + 1, section - 1)
    mirror = middle - 1 - base + (1 - half) * middle
    next_base = lax.rem(base + 1, middle)
    last_base = lax.rem(base + middle - 1, middle)
    is_first = base == 0
    is_last = base == middle - 1

    def remote(source, target, send, recv, **where):
        return pltpu.make_async_remote_copy(
            src_ref=source, dst_ref=target, send_sem=send, recv_sem=recv, device_id=where, device_id_type=MESH
        )

    def arrived(buffer, semaphore):
        remote(buffer, buffer, local_sem.at[0], semaphore, row=row).wait_recv()

    def each(low, high, action):
        def one(q, carry):
            action(q)
            return carry

        lax.fori_loop(low, high, one, 0)

    def inside(index):
        return jnp.logical_and(index >= 0, index < rows)

    def chunk(turn, shard, q):
        return matrix.at[turn, q, pl.ds(pl.multiple_of(shard * depth, 16), depth)]

    def own(q):
        return pltpu.make_async_copy(weight_ref.at[:, pl.ds(q * lanes, lanes)], chunk(half, row, q), own_sem.at[q])

    for q in range(blocks):
        own(q).start()
    fetch_latents = pltpu.make_async_copy(latent_hbm, latent_ref, local_sem.at[2])
    fetch_latents.start()
    fetch_taps = pltpu.make_async_copy(taps_hbm, taps_ref, local_sem.at[3])
    fetch_taps.start()
    fetch = pltpu.make_async_copy(table_hbm.at[0], table, local_sem.at[1])
    fetch.start()

    barrier = pltpu.get_barrier_semaphore()

    def greet(**where):
        pl.semaphore_signal(barrier, inc=1, device_id=where, device_id_type=MESH)

    reach = [d for d in range(1, rows) if d < rows - 1 or rows == 2]
    strides = sorted((sign * d for d in reach for sign in (1, -1)), key=lambda d: (abs(d) != 2, abs(d)))
    at_end = jnp.logical_or(row == 0, row == rows - 1)
    passes = jnp.logical_and(rows > 2, jnp.logical_or(row == 1, row == rows - 2))
    far = jnp.where(row == 1, rows - 1, 0)
    onto = jnp.where(row == 1, 0, rows - 1)

    expected = jnp.int32(0)
    for d in strides:

        @pl.when(inside(row + d))
        def _():
            greet(row=row + d)

        expected += inside(row + d).astype(jnp.int32)

    greet(section=partner)
    expected += 1
    for other_base in (next_base,) if middle == 2 else (next_base, last_base):
        for other_half in range(2):
            for other in range(cols):
                greet(section=other_base + other_half * middle, col=jnp.int32(other))
                expected += 1
    if middle > 2:
        greet(section=mirror)
        expected += 1

    @pl.when(is_first)
    def _():
        for hop in range(1, cols):
            greet(col=lax.rem(col + hop, cols))

    expected += (cols - 1) * is_first.astype(jnp.int32)
    pl.semaphore_wait(barrier, expected)

    for q in range(blocks):
        own(q).wait()

    def lend(q):
        return remote(
            chunk(half, row, q), chunk(half, row, q), lend_send.at[q], chunk_recv.at[half, row, q], section=partner
        )

    def latent_copy(m, hop):
        block = states.at[0, m, pl.ds(col * blocks, blocks)]
        return remote(
            block, block, latent_send.at[m, hop], state_recv.at[0, m, col * 2], col=lax.rem(col + hop, cols)
        )

    groups = tuple(part for part in ((0, kept), (kept, blocks)) if part[0] < part[1])

    def group(turn, part):
        low, high = groups[part]
        return lambda m: results.at[turn, m, pl.ds(low, high - low)]

    def state_copy(turn, part, m, other_half, hop):
        low, high = groups[part]
        later = jnp.where(is_last, 1, 0) if turn == 0 else 1
        return remote(
            group(turn, part)(m),
            states.at[later, m, pl.ds(col * blocks + low, high - low)],
            state_send.at[turn, m, other_half, hop],
            state_recv.at[later, m, col * 2 + part],
            section=next_base + other_half * middle,
            col=lax.rem(col + hop, cols),
        )

    def skip_copy(part, m):
        low, high = groups[part]
        return remote(
            group(0, part)(m), skips.at[m, pl.ds(low, high - low)], skip_send.at[m], skip_recv.at[m], section=mirror
        )

    def out_copy(turn, m):
        block = group(turn, 1)(m)
        return remote(block, block, out_send.at[m], out_recv.at[m], section=partner)

    def param_copy():
        return remote(params.at[half], params.at[half], param_send.at[0], param_recv.at[0], section=partner)

    def move(turn, d, q):
        block = chunk(turn, row, q)
        there = row + d
        return remote(
            block, block, chunk_send.at[turn, there, q], chunk_recv.at[turn, row, q], row=there
        )

    def forward(turn, q):
        block = chunk(turn, far, q)
        return remote(block, block, forward_send.at[turn, q], chunk_recv.at[turn, far, q], row=onto)

    def got(turn, shard, q):
        arrived(chunk(turn, shard, q), chunk_recv.at[turn, shard, q])

    def prepare():
        slot = lax.broadcasted_iota(jnp.int32, (16, steps), 0)
        number = lax.broadcasted_iota(jnp.int32, (16, steps), 1)
        chosen = jnp.zeros((16, steps), f32)
        for m in range(micro):
            hit = jnp.logical_and(slot == m, number == times_ref[m])
            chosen = jnp.where(hit, 1.0, chosen)
        fetch.wait()
        fetch_taps.wait()
        embedding = jnp.dot(chosen.astype(bf16), table[...], preferred_element_type=f32)
        for tap in range(3):
            params[half, tap : tap + 1, :] = 0.5 * taps_ref[tap]
        params[half, 3 : 3 + micro, :] = 0.5 * embedding[0:micro]
        params[half, 7:8, :] = jnp.full((1, cols * width), dilation_ref[0].astype(f32), f32)
        param_copy().start()

    def shift_of(turn):
        line = lax.broadcasted_iota(jnp.int32, (2 * frames, frames), 0).astype(f32)
        origin = lax.broadcasted_iota(jnp.int32, (2 * frames, frames), 1).astype(f32)
        dilation = params[turn, 7:8, 0:frames]
        wanted = jnp.where(line < frames, line - dilation, line - frames + dilation)
        shifts[turn] = jnp.where(origin == wanted, 1.0, 0.0).astype(bf16)

    def bounds(turn):
        helps = half != turn
        return helps, jnp.where(helps, kept, 0), jnp.where(helps, blocks, kept)

    def to_each(d, soon):
        to_end = jnp.logical_or(row + d == 0, row + d == rows - 1)
        first = jnp.where(at_end, abs(d) != 1, to_end)
        return jnp.logical_and(inside(row + d), first if soon else jnp.logical_not(first))

    def gather(turn):
        helps, low, high = bounds(turn)

        if turn == 0:

            @pl.when(parity == 1)
            def _():
                prepare()

                @pl.when(half == 0)
                def _():
                    each(kept, blocks, lambda q: lend(q).start())

        @pl.when(jnp.logical_or(turn > 0, parity == 1))
        def _():
            pl.semaphore_wait(turn_sem, 1)

        def first(q):
            @pl.when(helps)
            def _():
                got(turn, row, q)

            for d in strides:

                @pl.when(to_each(d, True))
                def _():
                    move(turn, d, q).start()

        each(low, high, first)

        if turn == 0:

            @pl.when(parity == 0)
            def _():
                prepare()

        def second(q):
            for d in strides:

                @pl.when(to_each(d, True))
                def _():
                    move(turn, d, q).wait_send()

            for d in strides:

                @pl.when(to_each(d, False))
                def _():
                    move(turn, d, q).start()

        each(low, high, second)

        @pl.when(jnp.logical_or(turn == 0, parity == 0))
        def _():
            pl.semaphore_signal(turn_sem, inc=1, device_id={"section": twin}, device_id_type=MESH)

        @pl.when(passes)
        def _():
            def onward(q):
                got(turn, far, q)
                forward(turn, q).start()

            each(low, high, onward)

        for hop in range(1, rows):
            shard = lax.rem(row + hop, rows)

            @pl.when(jnp.logical_not(jnp.logical_and(passes, shard == far)))
            def _():
                each(low, high, lambda q: got(turn, shard, q))

    def level(turn):
        helps, low, high = bounds(turn)

        @pl.when(helps)
        def _():
            arrived(params.at[turn], param_recv.at[0])

        shift_of(turn)

        def clip(m, carry):
            if turn == 0:

                @pl.when(is_first)
                def _():
                    for hop in range(1, cols):
                        other = lax.rem(col + hop, cols)
                        arrived(states.at[0, m, pl.ds(other * blocks, blocks)], state_recv.at[0, m, other * 2])

            for other in range(cols):
                for part, (low, high) in enumerate(groups):
                    span = states.at[turn, m, pl.ds(other * blocks + low, high - low)]
                    if turn == 0:

                        @pl.when(jnp.logical_not(is_first))
                        def _():
                            arrived(span, state_recv.at[0, m, other * 2 + part])

                    else:
                        arrived(span, state_recv.at[1, m, other * 2 + part])

            for g in range(cols * blocks):
                part = slice(g * lanes, (g + 1) * lanes)
                value = states[turn, m, g]
                moved = jnp.dot(shifts[turn], value, preferred_element_type=f32)
                pulse = params[turn, 3:4, part]
                for other in range(1, micro):
                    pulse = jnp.where(m == other, params[turn, 3 + other : 4 + other, part], pulse)
                vhalf = (
                    params[turn, 0:1, part] * moved[:frames]
                    + params[turn, 1:2, part] * value.astype(f32)
                    + params[turn, 2:3, part] * moved[frames:]
                    + pulse
                )
                active[:, part] = (vhalf + vhalf * jnp.tanh(vhalf)).astype(bf16)

            if turn == 1:

                @pl.when(is_first)
                def _():
                    for q in range(blocks):
                        skips[m, q] = states[1, m, col * blocks + q]

            def mix(part):
                low, high = groups[part]
                if turn == 1:

                    @pl.when(jnp.logical_not(is_first))
                    def _():
                        arrived(skips.at[m, pl.ds(low, high - low)], skip_recv.at[m])

                for q in range(low, high):
                    total = jnp.dot(active[...], matrix[turn, q], preferred_element_type=f32)
                    total = total + states[turn, m, col * blocks + q].astype(f32)
                    if turn == 1:
                        total = total + skips[m, q].astype(f32)
                    results[turn, m, q] = total.astype(bf16)

                @pl.when(jnp.logical_or(turn == 0, jnp.logical_not(is_last)))
                def _():
                    for away in (1, 0):
                        for hop in reversed(range(cols)):
                            state_copy(turn, part, m, lax.rem(half + away, 2), hop).start()

                if part == 1:
                    out_copy(turn, m).start()
                if turn == 0:

                    @pl.when(jnp.logical_not(is_last))
                    def _():
                        skip_copy(part, m).start()

            if len(groups) > 1:

                @pl.when(helps)
                def _():
                    mix(1)

            @pl.when(jnp.logical_not(helps))
            def _():
                mix(0)

            return carry

        lax.fori_loop(0, micro, clip, 0)

    @pl.when(jnp.logical_not(jnp.logical_and(parity == 1, half == 0)))
    def _():
        each(kept, blocks, lambda q: lend(q).start())

    fetch_latents.wait()

    @pl.when(is_first)
    def _():
        for m in range(micro):
            turned = latent_ref[m].astype(f32).T.astype(bf16)
            for q in range(blocks):
                states[0, m, col * blocks + q] = turned[:, q * lanes : (q + 1) * lanes]
            for hop in range(1, cols):
                latent_copy(m, hop).start()

    gather(0)
    level(0)
    gather(1)
    level(1)

    for m in range(micro):
        if len(groups) > 1:
            arrived(results.at[half, m, pl.ds(kept, blocks - kept)], out_recv.at[m])
        for q in range(blocks):
            out_ref[m, q * lanes : (q + 1) * lanes, :] = results[half, m, q].astype(f32).T.astype(bf16)

    each(kept, blocks, lambda q: lend(q).wait_send())
    param_copy().wait_send()

    @pl.when(is_first)
    def _():
        for m in range(micro):
            for hop in range(1, cols):
                latent_copy(m, hop).wait_send()

    for turn in range(2):
        helps, low, high = bounds(turn)

        def settle(q):
            for d in strides:

                @pl.when(to_each(d, False))
                def _():
                    move(turn, d, q).wait_send()

            @pl.when(passes)
            def _():
                forward(turn, q).wait_send()

        each(low, high, settle)

        def drain(part):
            for m in range(micro):

                @pl.when(jnp.logical_or(turn == 0, jnp.logical_not(is_last)))
                def _():
                    for other_half in range(2):
                        for hop in range(cols):
                            state_copy(turn, part, m, other_half, hop).wait_send()

                if part == 1:
                    out_copy(turn, m).wait_send()
                if turn == 0:

                    @pl.when(jnp.logical_not(is_last))
                    def _():
                        skip_copy(part, m).wait_send()

        if len(groups) > 1:

            @pl.when(helps)
            def _():
                drain(1)

        @pl.when(jnp.logical_not(helps))
        def _():
            drain(0)


def per_device(counts, latents, timesteps, weights, taps, time_table, dilations):
    sections, rows, cols = counts
    micro, width, _, frames = latents.shape
    depth = weights.shape[1]
    steps, channels = time_table.shape[1:]
    lanes = lanes_of(width)
    blocks = width // lanes
    bf16 = jnp.bfloat16
    dma = pltpu.SemaphoreType.DMA
    vmem = pl.BlockSpec(memory_space=pltpu.VMEM)
    smem = pl.BlockSpec(memory_space=pltpu.SMEM)
    hbm = pl.BlockSpec(memory_space=pl.ANY)
    out = pl.pallas_call(
        functools.partial(kernel, counts),
        out_shape=jax.ShapeDtypeStruct((micro, width, frames), bf16),
        in_specs=[smem, smem, hbm, hbm, hbm, hbm],
        out_specs=vmem,
        scratch_shapes=[
            pltpu.VMEM((2, blocks, channels, lanes), bf16),
            pltpu.VMEM((2, micro, cols * blocks, frames, lanes), bf16),
            pltpu.VMEM((frames, channels), bf16),
            pltpu.VMEM((2, micro, blocks, frames, lanes), bf16),
            pltpu.VMEM((micro, blocks, frames, lanes), bf16),
            pltpu.VMEM((2, 8, channels), jnp.float32),
            pltpu.VMEM((2, 2 * frames, frames), bf16),
            pltpu.VMEM((steps, channels), bf16),
            pltpu.VMEM((micro, width, frames), bf16),
            pltpu.VMEM((3, 1, channels), jnp.float32),
            dma((4,)),
            dma((blocks,)),
            pltpu.SemaphoreType.REGULAR,
            dma((2, rows, blocks)),
            dma((2, rows, blocks)),
            dma((2, blocks)),
            dma((blocks,)),
            dma((micro, cols)),
            dma((2, micro, 2, cols)),
            dma((2, micro, cols * 2)),
            dma((micro,)),
            dma((micro,)),
            dma((micro,)),
            dma((micro,)),
            dma((1,)),
            dma((1,)),
        ],
        compiler_params=pltpu.CompilerParams(
            collective_id=0, has_side_effects=True, vmem_limit_bytes=60 * 2**20
        ),
    )(
        timesteps,
        dilations,
        latents.reshape(micro, width, frames),
        weights,
        taps.reshape(3, 1, channels),
        time_table,
    )
    return out.reshape(1, micro, width, 1, frames)


def solution(mesh):
    counts = tuple(mesh.shape[axis] for axis in ("section", "row", "col"))
    in_specs = (
        P(None, "col", "row", None),
        P(),
        P("section", "row", "col"),
        P("section", None, None),
        P("section", None, None),
        P("section"),
    )
    return jax.shard_map(
        functools.partial(per_device, counts),
        mesh=mesh,
        in_specs=in_specs,
        out_specs=P("section", None, "col", "row", None),
        check_vma=False,
    )
```

```python
import functools

import jax
import jax.numpy as jnp
from jax import lax
from jax.experimental import pallas as pl
from jax.experimental.pallas import tpu as pltpu
from jax.sharding import PartitionSpec as P

MESH = pl.DeviceIdType.MESH


def lanes_of(width):
    return 128 if width % 128 == 0 else width


def kept_of(blocks):
    return -(-3 * blocks // 5)


def kernel(
    counts,
    times_ref,
    dilation_ref,
    latent_hbm,
    weight_hbm,
    taps_hbm,
    table_hbm,
    out_ref,
    matrix,
    states,
    active,
    results,
    skips,
    params,
    shifts,
    table,
    latent_ref,
    taps_ref,
    local_sem,
    own_sem,
    turn_sem,
    chunk_send,
    chunk_recv,
    forward_send,
    lend_send,
    latent_send,
    state_send,
    state_recv,
    skip_send,
    skip_recv,
    out_send,
    out_recv,
    param_send,
    param_recv,
):
    sections, rows, cols = counts
    section = lax.axis_index("section")
    row = lax.axis_index("row")
    col = lax.axis_index("col")
    micro, width, frames = latent_ref.shape
    weight_ref = weight_hbm.at[0]
    depth = weight_ref.shape[0]
    steps = table.shape[0]
    middle = sections // 2
    lanes = lanes_of(width)
    blocks = width // lanes
    kept = kept_of(blocks)
    f32 = jnp.float32
    bf16 = jnp.bfloat16

    half = section // middle
    base = lax.rem(section, middle)
    partner = lax.rem(section + middle, sections)
    parity = lax.rem(base, 2)
    twin = jnp.where(parity == 0, section + 1, section - 1)
    mirror = middle - 1 - base + (1 - half) * middle
    next_base = lax.rem(base + 1, middle)
    last_base = lax.rem(base + middle - 1, middle)
    is_first = base == 0
    is_last = base == middle - 1

    def remote(source, target, send, recv, **where):
        return pltpu.make_async_remote_copy(
            src_ref=source, dst_ref=target, send_sem=send, recv_sem=recv, device_id=where, device_id_type=MESH
        )

    def arrived(buffer, semaphore):
        remote(buffer, buffer, local_sem.at[0], semaphore, row=row).wait_recv()

    def each(low, high, action):
        def one(q, carry):
            action(q)
            return carry

        lax.fori_loop(low, high, one, 0)

    def inside(index):
        return jnp.logical_and(index >= 0, index < rows)

    def chunk(turn, shard, q):
        return matrix.at[turn, q, pl.ds(pl.multiple_of(shard * depth, 16), depth)]

    def own(q):
        return pltpu.make_async_copy(weight_ref.at[:, pl.ds(q * lanes, lanes)], chunk(half, row, q), own_sem.at[q])

    for q in reversed(range(blocks)):
        own(q).start()
    fetch_latents = pltpu.make_async_copy(latent_hbm, latent_ref, local_sem.at[2])
    fetch_latents.start()
    fetch_taps = pltpu.make_async_copy(taps_hbm, taps_ref, local_sem.at[3])
    fetch_taps.start()
    fetch = pltpu.make_async_copy(table_hbm.at[0], table, local_sem.at[1])
    fetch.start()

    barrier = pltpu.get_barrier_semaphore()

    def greet(**where):
        pl.semaphore_signal(barrier, inc=1, device_id=where, device_id_type=MESH)

    reach = [d for d in range(1, rows) if d < rows - 1 or rows == 2]
    strides = sorted((sign * d for d in reach for sign in (1, -1)), key=lambda d: (abs(d) != 2, abs(d)))
    at_end = jnp.logical_or(row == 0, row == rows - 1)
    passes = jnp.logical_and(rows > 2, jnp.logical_or(row == 1, row == rows - 2))
    far = jnp.where(row == 1, rows - 1, 0)
    onto = jnp.where(row == 1, 0, rows - 1)

    expected = jnp.int32(0)
    for d in strides:

        @pl.when(inside(row + d))
        def _():
            greet(row=row + d)

        expected += inside(row + d).astype(jnp.int32)

    greet(section=partner)
    expected += 1
    for other_base in (next_base,) if middle == 2 else (next_base, last_base):
        for other_half in range(2):
            for other in range(cols):
                greet(section=other_base + other_half * middle, col=jnp.int32(other))
                expected += 1
    if middle > 2:
        greet(section=mirror)
        expected += 1

    @pl.when(is_first)
    def _():
        for hop in range(1, cols):
            greet(col=lax.rem(col + hop, cols))

    expected += (cols - 1) * is_first.astype(jnp.int32)
    pl.semaphore_wait(barrier, expected)

    for q in range(kept, blocks):
        own(q).wait()

    def lend(q):
        return remote(
            chunk(half, row, q), chunk(half, row, q), lend_send.at[q], chunk_recv.at[half, row, q], section=partner
        )

    def latent_copy(m, hop):
        block = states.at[0, m, pl.ds(col * blocks, blocks)]
        return remote(
            block, block, latent_send.at[m, hop], state_recv.at[0, m, col * 2], col=lax.rem(col + hop, cols)
        )

    groups = tuple(part for part in ((0, kept), (kept, blocks)) if part[0] < part[1])

    def group(turn, part):
        low, high = groups[part]
        return lambda m: results.at[turn, m, pl.ds(low, high - low)]

    def state_copy(turn, part, m, other_half, hop):
        low, high = groups[part]
        later = jnp.where(is_last, 1, 0) if turn == 0 else 1
        return remote(
            group(turn, part)(m),
            states.at[later, m, pl.ds(col * blocks + low, high - low)],
            state_send.at[turn, m, other_half, hop],
            state_recv.at[later, m, col * 2 + part],
            section=next_base + other_half * middle,
            col=lax.rem(col + hop, cols),
        )

    def skip_copy(part, m):
        low, high = groups[part]
        return remote(
            group(0, part)(m), skips.at[m, pl.ds(low, high - low)], skip_send.at[m], skip_recv.at[m], section=mirror
        )

    def out_copy(turn, m):
        block = group(turn, 1)(m)
        return remote(block, block, out_send.at[m], out_recv.at[m], section=partner)

    def param_copy():
        return remote(params.at[half], params.at[half], param_send.at[0], param_recv.at[0], section=partner)

    def move(turn, d, q):
        block = chunk(turn, row, q)
        there = row + d
        return remote(
            block, block, chunk_send.at[turn, there, q], chunk_recv.at[turn, row, q], row=there
        )

    def forward(turn, q):
        block = chunk(turn, far, q)
        return remote(block, block, forward_send.at[turn, q], chunk_recv.at[turn, far, q], row=onto)

    def got(turn, shard, q):
        arrived(chunk(turn, shard, q), chunk_recv.at[turn, shard, q])

    def prepare():
        slot = lax.broadcasted_iota(jnp.int32, (16, steps), 0)
        number = lax.broadcasted_iota(jnp.int32, (16, steps), 1)
        chosen = jnp.zeros((16, steps), f32)
        for m in range(micro):
            hit = jnp.logical_and(slot == m, number == times_ref[m])
            chosen = jnp.where(hit, 1.0, chosen)
        fetch.wait()
        fetch_taps.wait()
        embedding = jnp.dot(chosen.astype(bf16), table[...], preferred_element_type=f32)
        for tap in range(3):
            params[half, tap : tap + 1, :] = 0.5 * taps_ref[tap]
        params[half, 3 : 3 + micro, :] = 0.5 * embedding[0:micro]
        params[half, 7:8, :] = jnp.full((1, cols * width), dilation_ref[0].astype(f32), f32)
        param_copy().start()

    def shift_of(turn):
        line = lax.broadcasted_iota(jnp.int32, (2 * frames, frames), 0).astype(f32)
        origin = lax.broadcasted_iota(jnp.int32, (2 * frames, frames), 1).astype(f32)
        dilation = params[turn, 7:8, 0:frames]
        wanted = jnp.where(line < frames, line - dilation, line - frames + dilation)
        shifts[turn] = jnp.where(origin == wanted, 1.0, 0.0).astype(bf16)

    def bounds(turn):
        helps = half != turn
        return helps, jnp.where(helps, kept, 0), jnp.where(helps, blocks, kept)

    def spread():
        fetch_latents.wait()

        @pl.when(is_first)
        def _():
            for m in range(micro):
                turned = latent_ref[m].astype(f32).T.astype(bf16)
                for q in range(blocks):
                    states[0, m, col * blocks + q] = turned[:, q * lanes : (q + 1) * lanes]
                for hop in range(1, cols):
                    latent_copy(m, hop).start()

    def to_each(d, soon):
        to_end = jnp.logical_or(row + d == 0, row + d == rows - 1)
        first = jnp.where(at_end, abs(d) != 1, to_end)
        return jnp.logical_and(inside(row + d), first if soon else jnp.logical_not(first))

    def gather(turn):
        helps, low, high = bounds(turn)

        if turn == 0:

            @pl.when(parity == 1)
            def _():
                prepare()

                @pl.when(half == 0)
                def _():
                    each(kept, blocks, lambda q: lend(q).start())

        @pl.when(jnp.logical_or(turn > 0, parity == 1))
        def _():
            pl.semaphore_wait(turn_sem, 1)

        def first(q):
            @pl.when(helps)
            def _():
                got(turn, row, q)

            for d in strides:

                @pl.when(to_each(d, True))
                def _():
                    move(turn, d, q).start()

        each(low, high, first)

        if turn == 0:
            spread()

        if turn == 0:

            @pl.when(parity == 0)
            def _():
                prepare()

        def second(q):
            for d in strides:

                @pl.when(to_each(d, True))
                def _():
                    move(turn, d, q).wait_send()

            for d in strides:

                @pl.when(to_each(d, False))
                def _():
                    move(turn, d, q).start()

        each(low, high, second)

        @pl.when(jnp.logical_or(turn == 0, parity == 0))
        def _():
            pl.semaphore_signal(turn_sem, inc=1, device_id={"section": twin}, device_id_type=MESH)

        @pl.when(passes)
        def _():
            def onward(q):
                got(turn, far, q)
                forward(turn, q).start()

            each(low, high, onward)

        for hop in range(1, rows):
            shard = lax.rem(row + hop, rows)

            @pl.when(jnp.logical_not(jnp.logical_and(passes, shard == far)))
            def _():
                each(low, high, lambda q: got(turn, shard, q))

    def level(turn):
        helps, low, high = bounds(turn)

        @pl.when(helps)
        def _():
            arrived(params.at[turn], param_recv.at[0])

        shift_of(turn)

        def clip(m, carry):
            if turn == 0:

                @pl.when(is_first)
                def _():
                    for hop in range(1, cols):
                        other = lax.rem(col + hop, cols)
                        arrived(states.at[0, m, pl.ds(other * blocks, blocks)], state_recv.at[0, m, other * 2])

            for other in range(cols):
                for part, (low, high) in enumerate(groups):
                    span = states.at[turn, m, pl.ds(other * blocks + low, high - low)]
                    if turn == 0:

                        @pl.when(jnp.logical_not(is_first))
                        def _():
                            arrived(span, state_recv.at[0, m, other * 2 + part])

                    else:
                        arrived(span, state_recv.at[1, m, other * 2 + part])

            for g in range(cols * blocks):
                part = slice(g * lanes, (g + 1) * lanes)
                value = states[turn, m, g]
                moved = jnp.dot(shifts[turn], value, preferred_element_type=f32)
                pulse = params[turn, 3:4, part]
                for other in range(1, micro):
                    pulse = jnp.where(m == other, params[turn, 3 + other : 4 + other, part], pulse)
                vhalf = (
                    params[turn, 0:1, part] * moved[:frames]
                    + params[turn, 1:2, part] * value.astype(f32)
                    + params[turn, 2:3, part] * moved[frames:]
                    + pulse
                )
                active[:, part] = (vhalf + vhalf * jnp.tanh(vhalf)).astype(bf16)

            if turn == 1:

                @pl.when(is_first)
                def _():
                    for q in range(blocks):
                        skips[m, q] = states[1, m, col * blocks + q]

            def mix(part):
                low, high = groups[part]
                if turn == 1:

                    @pl.when(jnp.logical_not(is_first))
                    def _():
                        arrived(skips.at[m, pl.ds(low, high - low)], skip_recv.at[m])

                for q in range(low, high):
                    total = jnp.dot(active[...], matrix[turn, q], preferred_element_type=f32)
                    total = total + states[turn, m, col * blocks + q].astype(f32)
                    if turn == 1:
                        total = total + skips[m, q].astype(f32)
                    results[turn, m, q] = total.astype(bf16)

                @pl.when(jnp.logical_or(turn == 0, jnp.logical_not(is_last)))
                def _():
                    for away in (1, 0):
                        for hop in reversed(range(cols)):
                            state_copy(turn, part, m, lax.rem(half + away, 2), hop).start()

                if part == 1:
                    out_copy(turn, m).start()
                if turn == 0:

                    @pl.when(jnp.logical_not(is_last))
                    def _():
                        skip_copy(part, m).start()

            if len(groups) > 1:

                @pl.when(helps)
                def _():
                    mix(1)

            @pl.when(jnp.logical_not(helps))
            def _():
                mix(0)

            return carry

        lax.fori_loop(0, micro, clip, 0)

    @pl.when(jnp.logical_not(jnp.logical_and(parity == 1, half == 0)))
    def _():
        each(kept, blocks, lambda q: lend(q).start())

    for q in range(kept):
        own(q).wait()

    gather(0)
    level(0)
    gather(1)
    level(1)

    for m in range(micro):
        if len(groups) > 1:
            arrived(results.at[half, m, pl.ds(kept, blocks - kept)], out_recv.at[m])
        for q in range(blocks):
            out_ref[m, q * lanes : (q + 1) * lanes, :] = results[half, m, q].astype(f32).T.astype(bf16)

    each(kept, blocks, lambda q: lend(q).wait_send())
    param_copy().wait_send()

    @pl.when(is_first)
    def _():
        for m in range(micro):
            for hop in range(1, cols):
                latent_copy(m, hop).wait_send()

    for turn in range(2):
        helps, low, high = bounds(turn)

        def settle(q):
            for d in strides:

                @pl.when(to_each(d, False))
                def _():
                    move(turn, d, q).wait_send()

            @pl.when(passes)
            def _():
                forward(turn, q).wait_send()

        each(low, high, settle)

        def drain(part):
            for m in range(micro):

                @pl.when(jnp.logical_or(turn == 0, jnp.logical_not(is_last)))
                def _():
                    for other_half in range(2):
                        for hop in range(cols):
                            state_copy(turn, part, m, other_half, hop).wait_send()

                if part == 1:
                    out_copy(turn, m).wait_send()
                if turn == 0:

                    @pl.when(jnp.logical_not(is_last))
                    def _():
                        skip_copy(part, m).wait_send()

        if len(groups) > 1:

            @pl.when(helps)
            def _():
                drain(1)

        @pl.when(jnp.logical_not(helps))
        def _():
            drain(0)


def per_device(counts, latents, timesteps, weights, taps, time_table, dilations):
    sections, rows, cols = counts
    micro, width, _, frames = latents.shape
    depth = weights.shape[1]
    steps, channels = time_table.shape[1:]
    lanes = lanes_of(width)
    blocks = width // lanes
    bf16 = jnp.bfloat16
    dma = pltpu.SemaphoreType.DMA
    vmem = pl.BlockSpec(memory_space=pltpu.VMEM)
    smem = pl.BlockSpec(memory_space=pltpu.SMEM)
    hbm = pl.BlockSpec(memory_space=pl.ANY)
    out = pl.pallas_call(
        functools.partial(kernel, counts),
        out_shape=jax.ShapeDtypeStruct((micro, width, frames), bf16),
        in_specs=[smem, smem, hbm, hbm, hbm, hbm],
        out_specs=vmem,
        scratch_shapes=[
            pltpu.VMEM((2, blocks, channels, lanes), bf16),
            pltpu.VMEM((2, micro, cols * blocks, frames, lanes), bf16),
            pltpu.VMEM((frames, channels), bf16),
            pltpu.VMEM((2, micro, blocks, frames, lanes), bf16),
            pltpu.VMEM((micro, blocks, frames, lanes), bf16),
            pltpu.VMEM((2, 8, channels), jnp.float32),
            pltpu.VMEM((2, 2 * frames, frames), bf16),
            pltpu.VMEM((steps, channels), bf16),
            pltpu.VMEM((micro, width, frames), bf16),
            pltpu.VMEM((3, 1, channels), jnp.float32),
            dma((4,)),
            dma((blocks,)),
            pltpu.SemaphoreType.REGULAR,
            dma((2, rows, blocks)),
            dma((2, rows, blocks)),
            dma((2, blocks)),
            dma((blocks,)),
            dma((micro, cols)),
            dma((2, micro, 2, cols)),
            dma((2, micro, cols * 2)),
            dma((micro,)),
            dma((micro,)),
            dma((micro,)),
            dma((micro,)),
            dma((1,)),
            dma((1,)),
        ],
        compiler_params=pltpu.CompilerParams(
            collective_id=0, has_side_effects=True, vmem_limit_bytes=60 * 2**20
        ),
    )(
        timesteps,
        dilations,
        latents.reshape(micro, width, frames),
        weights,
        taps.reshape(3, 1, channels),
        time_table,
    )
    return out.reshape(1, micro, width, 1, frames)


def solution(mesh):
    counts = tuple(mesh.shape[axis] for axis in ("section", "row", "col"))
    in_specs = (
        P(None, "col", "row", None),
        P(),
        P("section", "row", "col"),
        P("section", None, None),
        P("section", None, None),
        P("section"),
    )
    return jax.shard_map(
        functools.partial(per_device, counts),
        mesh=mesh,
        in_specs=in_specs,
        out_specs=P("section", None, "col", "row", None),
        check_vma=False,
    )
```

```python
import functools

import jax
import jax.numpy as jnp
from jax import lax
from jax.experimental import pallas as pl
from jax.experimental.pallas import tpu as pltpu
from jax.sharding import PartitionSpec as P

MESH = pl.DeviceIdType.MESH


def lanes_of(width):
    return 128 if width % 128 == 0 else width


def kept_of(blocks):
    return -(-3 * blocks // 5)


def kernel(
    counts,
    times_ref,
    dilation_ref,
    latent_hbm,
    weight_hbm,
    taps_hbm,
    table_hbm,
    out_ref,
    matrix,
    states,
    active,
    results,
    skips,
    params,
    shifts,
    table,
    latent_ref,
    taps_ref,
    local_sem,
    own_sem,
    turn_sem,
    chunk_send,
    chunk_recv,
    forward_send,
    lend_send,
    latent_send,
    state_send,
    state_recv,
    skip_send,
    skip_recv,
    out_send,
    out_recv,
    param_send,
    param_recv,
):
    sections, rows, cols = counts
    section = lax.axis_index("section")
    row = lax.axis_index("row")
    col = lax.axis_index("col")
    micro, width, frames = latent_ref.shape
    weight_ref = weight_hbm.at[0]
    depth = weight_ref.shape[0]
    steps = table.shape[0]
    middle = sections // 2
    lanes = lanes_of(width)
    blocks = width // lanes
    kept = kept_of(blocks)
    f32 = jnp.float32
    bf16 = jnp.bfloat16

    half = section // middle
    base = lax.rem(section, middle)
    partner = lax.rem(section + middle, sections)
    parity = lax.rem(base, 2)
    twin = jnp.where(parity == 0, section + 1, section - 1)
    mirror = middle - 1 - base + (1 - half) * middle
    next_base = lax.rem(base + 1, middle)
    last_base = lax.rem(base + middle - 1, middle)
    is_first = base == 0
    is_last = base == middle - 1

    def remote(source, target, send, recv, **where):
        return pltpu.make_async_remote_copy(
            src_ref=source, dst_ref=target, send_sem=send, recv_sem=recv, device_id=where, device_id_type=MESH
        )

    def arrived(buffer, semaphore):
        remote(buffer, buffer, local_sem.at[0], semaphore, row=row).wait_recv()

    def each(low, high, action):
        def one(q, carry):
            action(q)
            return carry

        lax.fori_loop(low, high, one, 0)

    def inside(index):
        return jnp.logical_and(index >= 0, index < rows)

    def chunk(turn, shard, q):
        return matrix.at[turn, q, pl.ds(pl.multiple_of(shard * depth, 16), depth)]

    def own(q):
        return pltpu.make_async_copy(weight_ref.at[:, pl.ds(q * lanes, lanes)], chunk(half, row, q), own_sem.at[q])

    for q in reversed(range(blocks)):
        own(q).start()
    fetch_latents = pltpu.make_async_copy(latent_hbm, latent_ref, local_sem.at[2])
    fetch_latents.start()
    fetch_taps = pltpu.make_async_copy(taps_hbm, taps_ref, local_sem.at[3])
    fetch_taps.start()
    fetch = pltpu.make_async_copy(table_hbm.at[0], table, local_sem.at[1])
    fetch.start()

    barrier = pltpu.get_barrier_semaphore()

    def greet(**where):
        pl.semaphore_signal(barrier, inc=1, device_id=where, device_id_type=MESH)

    reach = [d for d in range(1, rows) if d < rows - 1 or rows == 2]
    strides = sorted((sign * d for d in reach for sign in (1, -1)), key=lambda d: (abs(d) != 2, abs(d)))
    at_end = jnp.logical_or(row == 0, row == rows - 1)
    passes = jnp.logical_and(rows > 2, jnp.logical_or(row == 1, row == rows - 2))
    far = jnp.where(row == 1, rows - 1, 0)
    onto = jnp.where(row == 1, 0, rows - 1)

    expected = jnp.int32(0)
    for d in strides:

        @pl.when(inside(row + d))
        def _():
            greet(row=row + d)

        expected += inside(row + d).astype(jnp.int32)

    greet(section=partner)
    expected += 1
    for other_base in (next_base,) if middle == 2 else (next_base, last_base):
        for other_half in range(2):
            for other in range(cols):
                greet(section=other_base + other_half * middle, col=jnp.int32(other))
                expected += 1
    if middle > 2:
        greet(section=mirror)
        expected += 1

    @pl.when(is_first)
    def _():
        for hop in range(1, cols):
            greet(col=lax.rem(col + hop, cols))

    expected += (cols - 1) * is_first.astype(jnp.int32)
    pl.semaphore_wait(barrier, expected)

    for q in range(kept, blocks):
        own(q).wait()

    def lend(q):
        return remote(
            chunk(half, row, q), chunk(half, row, q), lend_send.at[q], chunk_recv.at[half, row, q], section=partner
        )

    def latent_copy(m, hop):
        block = states.at[0, m, pl.ds(col * blocks, blocks)]
        return remote(
            block, block, latent_send.at[m, hop], state_recv.at[0, m, col * 2], col=lax.rem(col + hop, cols)
        )

    groups = tuple(part for part in ((0, kept), (kept, blocks)) if part[0] < part[1])

    def group(turn, part):
        low, high = groups[part]
        return lambda m: results.at[turn, m, pl.ds(low, high - low)]

    def state_copy(turn, part, m, other_half, hop):
        low, high = groups[part]
        later = jnp.where(is_last, 1, 0) if turn == 0 else 1
        return remote(
            group(turn, part)(m),
            states.at[later, m, pl.ds(col * blocks + low, high - low)],
            state_send.at[turn, m, other_half, hop],
            state_recv.at[later, m, col * 2 + part],
            section=next_base + other_half * middle,
            col=lax.rem(col + hop, cols),
        )

    def skip_copy(part, m):
        low, high = groups[part]
        return remote(
            group(0, part)(m), skips.at[m, pl.ds(low, high - low)], skip_send.at[m], skip_recv.at[m], section=mirror
        )

    def out_copy(turn, m):
        block = group(turn, 1)(m)
        return remote(block, block, out_send.at[m], out_recv.at[m], section=partner)

    def param_copy():
        return remote(params.at[half], params.at[half], param_send.at[0], param_recv.at[0], section=partner)

    def move(turn, d, q):
        block = chunk(turn, row, q)
        there = row + d
        return remote(
            block, block, chunk_send.at[turn, there, q], chunk_recv.at[turn, row, q], row=there
        )

    def forward(turn, q):
        block = chunk(turn, far, q)
        return remote(block, block, forward_send.at[turn, q], chunk_recv.at[turn, far, q], row=onto)

    def got(turn, shard, q):
        arrived(chunk(turn, shard, q), chunk_recv.at[turn, shard, q])

    def prepare():
        slot = lax.broadcasted_iota(jnp.int32, (16, steps), 0)
        number = lax.broadcasted_iota(jnp.int32, (16, steps), 1)
        chosen = jnp.zeros((16, steps), f32)
        for m in range(micro):
            hit = jnp.logical_and(slot == m, number == times_ref[m])
            chosen = jnp.where(hit, 1.0, chosen)
        fetch.wait()
        fetch_taps.wait()
        embedding = jnp.dot(chosen.astype(bf16), table[...], preferred_element_type=f32)
        for tap in range(3):
            params[half, tap : tap + 1, :] = 0.5 * taps_ref[tap]
        params[half, 3 : 3 + micro, :] = 0.5 * embedding[0:micro]
        params[half, 7:8, :] = jnp.full((1, cols * width), dilation_ref[0].astype(f32), f32)
        param_copy().start()

    def shift_of(turn):
        line = lax.broadcasted_iota(jnp.int32, (2 * frames, frames), 0).astype(f32)
        origin = lax.broadcasted_iota(jnp.int32, (2 * frames, frames), 1).astype(f32)
        dilation = params[turn, 7:8, 0:frames]
        wanted = jnp.where(line < frames, line - dilation, line - frames + dilation)
        shifts[turn] = jnp.where(origin == wanted, 1.0, 0.0).astype(bf16)

    def bounds(turn):
        helps = half != turn
        return helps, jnp.where(helps, kept, 0), jnp.where(helps, blocks, kept)

    def spread():
        fetch_latents.wait()

        @pl.when(is_first)
        def _():
            for m in range(micro):
                turned = latent_ref[m].astype(f32).T.astype(bf16)
                for q in range(blocks):
                    states[0, m, col * blocks + q] = turned[:, q * lanes : (q + 1) * lanes]
                for hop in range(1, cols):
                    latent_copy(m, hop).start()

    def to_each(d, soon):
        to_end = jnp.logical_or(row + d == 0, row + d == rows - 1)
        first = jnp.where(at_end, abs(d) != 1, to_end)
        return jnp.logical_and(inside(row + d), first if soon else jnp.logical_not(first))

    def gather(turn):
        helps, low, high = bounds(turn)

        if turn == 0:

            @pl.when(parity == 1)
            def _():
                prepare()

                @pl.when(half == 0)
                def _():
                    each(kept, blocks, lambda q: lend(q).start())

        @pl.when(jnp.logical_or(turn > 0, parity == 1))
        def _():
            pl.semaphore_wait(turn_sem, 1)

        def first(q):
            @pl.when(helps)
            def _():
                got(turn, row, q)

            for d in strides:

                @pl.when(to_each(d, True))
                def _():
                    move(turn, d, q).start()

        each(low, high, first)

        if turn == 0:
            spread()

        if turn == 0:

            @pl.when(parity == 0)
            def _():
                prepare()

        def second(q):
            for d in strides:

                @pl.when(to_each(d, True))
                def _():
                    move(turn, d, q).wait_send()

            for d in strides:

                @pl.when(to_each(d, False))
                def _():
                    move(turn, d, q).start()

        each(low, high, second)

        @pl.when(jnp.logical_or(turn == 0, parity == 0))
        def _():
            pl.semaphore_signal(turn_sem, inc=1, device_id={"section": twin}, device_id_type=MESH)

        @pl.when(passes)
        def _():
            def onward(q):
                got(turn, far, q)
                forward(turn, q).start()

            each(low, high, onward)

        for hop in range(1, rows):
            shard = lax.rem(row + hop, rows)

            @pl.when(jnp.logical_not(jnp.logical_and(passes, shard == far)))
            def _():
                each(low, high, lambda q: got(turn, shard, q))

    def level(turn):
        helps, low, high = bounds(turn)

        @pl.when(helps)
        def _():
            arrived(params.at[turn], param_recv.at[0])

        shift_of(turn)

        def clip(m, carry):
            if turn == 0:

                @pl.when(is_first)
                def _():
                    for hop in range(1, cols):
                        other = lax.rem(col + hop, cols)
                        arrived(states.at[0, m, pl.ds(other * blocks, blocks)], state_recv.at[0, m, other * 2])

            for other in range(cols):
                for part, (low, high) in enumerate(groups):
                    span = states.at[turn, m, pl.ds(other * blocks + low, high - low)]
                    if turn == 0:

                        @pl.when(jnp.logical_not(is_first))
                        def _():
                            arrived(span, state_recv.at[0, m, other * 2 + part])

                    else:
                        arrived(span, state_recv.at[1, m, other * 2 + part])

            for g in range(cols * blocks):
                part = slice(g * lanes, (g + 1) * lanes)
                value = states[turn, m, g]
                moved = jnp.dot(shifts[turn], value, preferred_element_type=f32)
                pulse = params[turn, 3:4, part]
                for other in range(1, micro):
                    pulse = jnp.where(m == other, params[turn, 3 + other : 4 + other, part], pulse)
                vhalf = (
                    params[turn, 0:1, part] * moved[:frames]
                    + params[turn, 1:2, part] * value.astype(f32)
                    + params[turn, 2:3, part] * moved[frames:]
                    + pulse
                )
                active[:, part] = (vhalf + vhalf * jnp.tanh(vhalf)).astype(bf16)

            if turn == 1:

                @pl.when(is_first)
                def _():
                    for q in range(blocks):
                        skips[m, q] = states[1, m, col * blocks + q]

            def mix(part):
                low, high = groups[part]
                if turn == 1:

                    @pl.when(jnp.logical_not(is_first))
                    def _():
                        arrived(skips.at[m, pl.ds(low, high - low)], skip_recv.at[m])

                for q in range(low, high):
                    total = jnp.dot(active[...], matrix[turn, q], preferred_element_type=f32)
                    total = total + states[turn, m, col * blocks + q].astype(f32)
                    if turn == 1:
                        total = total + skips[m, q].astype(f32)
                    results[turn, m, q] = total.astype(bf16)

                @pl.when(jnp.logical_or(turn == 0, jnp.logical_not(is_last)))
                def _():
                    for away in (1, 0):
                        for hop in reversed(range(cols)):
                            state_copy(turn, part, m, lax.rem(half + away, 2), hop).start()

                if part == 1:
                    out_copy(turn, m).start()
                if turn == 0:

                    @pl.when(jnp.logical_not(is_last))
                    def _():
                        skip_copy(part, m).start()

            if len(groups) > 1:

                @pl.when(helps)
                def _():
                    mix(1)

            @pl.when(jnp.logical_not(helps))
            def _():
                mix(0)

            return carry

        lax.fori_loop(0, micro, clip, 0)

    @pl.when(jnp.logical_not(jnp.logical_and(parity == 1, half == 0)))
    def _():
        each(kept, blocks, lambda q: lend(q).start())

    for q in range(kept):
        own(q).wait()

    gather(0)
    level(0)
    gather(1)
    level(1)

    for m in range(micro):
        if len(groups) > 1:
            arrived(results.at[half, m, pl.ds(kept, blocks - kept)], out_recv.at[m])
        for q in range(blocks):
            out_ref[m, q] = results[half, m, q]

    each(kept, blocks, lambda q: lend(q).wait_send())
    param_copy().wait_send()

    @pl.when(is_first)
    def _():
        for m in range(micro):
            for hop in range(1, cols):
                latent_copy(m, hop).wait_send()

    for turn in range(2):
        helps, low, high = bounds(turn)

        def settle(q):
            for d in strides:

                @pl.when(to_each(d, False))
                def _():
                    move(turn, d, q).wait_send()

            @pl.when(passes)
            def _():
                forward(turn, q).wait_send()

        each(low, high, settle)

        def drain(part):
            for m in range(micro):

                @pl.when(jnp.logical_or(turn == 0, jnp.logical_not(is_last)))
                def _():
                    for other_half in range(2):
                        for hop in range(cols):
                            state_copy(turn, part, m, other_half, hop).wait_send()

                if part == 1:
                    out_copy(turn, m).wait_send()
                if turn == 0:

                    @pl.when(jnp.logical_not(is_last))
                    def _():
                        skip_copy(part, m).wait_send()

        if len(groups) > 1:

            @pl.when(helps)
            def _():
                drain(1)

        @pl.when(jnp.logical_not(helps))
        def _():
            drain(0)


def per_device(counts, latents, timesteps, weights, taps, time_table, dilations):
    sections, rows, cols = counts
    micro, width, _, frames = latents.shape
    depth = weights.shape[1]
    steps, channels = time_table.shape[1:]
    lanes = lanes_of(width)
    blocks = width // lanes
    bf16 = jnp.bfloat16
    dma = pltpu.SemaphoreType.DMA
    vmem = pl.BlockSpec(memory_space=pltpu.VMEM)
    smem = pl.BlockSpec(memory_space=pltpu.SMEM)
    hbm = pl.BlockSpec(memory_space=pl.ANY)
    out = pl.pallas_call(
        functools.partial(kernel, counts),
        out_shape=jax.ShapeDtypeStruct((micro, blocks, frames, lanes), bf16),
        in_specs=[smem, smem, hbm, hbm, hbm, hbm],
        out_specs=vmem,
        scratch_shapes=[
            pltpu.VMEM((2, blocks, channels, lanes), bf16),
            pltpu.VMEM((2, micro, cols * blocks, frames, lanes), bf16),
            pltpu.VMEM((frames, channels), bf16),
            pltpu.VMEM((2, micro, blocks, frames, lanes), bf16),
            pltpu.VMEM((micro, blocks, frames, lanes), bf16),
            pltpu.VMEM((2, 8, channels), jnp.float32),
            pltpu.VMEM((2, 2 * frames, frames), bf16),
            pltpu.VMEM((steps, channels), bf16),
            pltpu.VMEM((micro, width, frames), bf16),
            pltpu.VMEM((3, 1, channels), jnp.float32),
            dma((4,)),
            dma((blocks,)),
            pltpu.SemaphoreType.REGULAR,
            dma((2, rows, blocks)),
            dma((2, rows, blocks)),
            dma((2, blocks)),
            dma((blocks,)),
            dma((micro, cols)),
            dma((2, micro, 2, cols)),
            dma((2, micro, cols * 2)),
            dma((micro,)),
            dma((micro,)),
            dma((micro,)),
            dma((micro,)),
            dma((1,)),
            dma((1,)),
        ],
        compiler_params=pltpu.CompilerParams(
            collective_id=0, has_side_effects=True, vmem_limit_bytes=60 * 2**20
        ),
    )(
        timesteps,
        dilations,
        latents.reshape(micro, width, frames),
        weights,
        taps.reshape(3, 1, channels),
        time_table,
    )
    return out.swapaxes(2, 3).reshape(1, micro, width, 1, frames)


def solution(mesh):
    counts = tuple(mesh.shape[axis] for axis in ("section", "row", "col"))
    in_specs = (
        P(None, "col", "row", None),
        P(),
        P("section", "row", "col"),
        P("section", None, None),
        P("section", None, None),
        P("section"),
    )
    return jax.shard_map(
        functools.partial(per_device, counts),
        mesh=mesh,
        in_specs=in_specs,
        out_specs=P("section", None, "col", "row", None),
        check_vma=False,
    )
```
